512 devices in a mesh: tiles: 128 (over z, y, core), rep: 4 (over x).
Axes of the slice: x: 4, y: 8, z: 8, core: 2. Of those that a mesh axis runs over, the one named last changes fastest.
Arguments:
- tile_embed: bfloat16 [4, 896, 128, 1280], P('rep', 'tiles'), may hold values from -24 to 24
- block_slide: int32 [4, 896], P('rep', 'tiles'), may hold values from -1 to 0, as said below
- block_rank: int32 [4, 896], P('rep', 'tiles'), may hold values from 0 to 895, as said below
- tile_count: int32 [4, 1], P('rep'), may hold values from 1 to 114688, as said below
- queries: bfloat16 [64, 640], replicated, may hold values from -160 to 160
- w_key: bfloat16 [1280, 640], P('rep'), may hold values from -0.2 to 0.2
- w_value: bfloat16 [1280, 640], P('rep'), may hold values from -0.15625 to 0.15625
- d_attended: bfloat16 [4, 1, 64, 640], P('rep'), may hold values from -6 to 6
Outputs:
- attended: bfloat16 [4, 1, 64, 640], P('rep')
- key_grad: float32 [1280, 640], P('tiles', 'rep')
- value_grad: float32 [1280, 640], P('tiles', 'rep')
The draws below stay inside these ranges and needn't reach their ends.
Inputs may be any that keep to these rules, and one draw needn't show every extreme that they name: `block_slide`: each device's live blocks fill its first slots and the others hold -1; a device has between 5 and 7 live blocks, both ends reached on some device of every group; every slide has at least one block. `block_rank`: A slide with n blocks in its group holds each rank 0 to n - 1 exactly once; empty slots hold 0. `tile_count`: A slide with n blocks has more than 128 * (n - 1) tiles and at most 128 * n.
All inputs are finite; a program needn't handle non-finite values.
Results may differ from the reference program's by a relative error of at most 0.019.
The reference program's roundings to bfloat16 on the way count: a program that leaves them out, or rounds other values in their place, can miss the bound.
Values may be sent and summed in bfloat16 or wider, within the bound.
No kernel may reach another device: no remote copies, remote signals or barrier semaphores. Data moves between devices by JAX's collectives and lax.ppermute only.
A program may use at most 128 MiB of HBM per device.

```python
import math
import jax
import jax.numpy as jnp
from jax import lax

D_IN = 1280
HEADS = 10
HEAD_DIM = 64
LATENTS = 64
TILE_ROWS = 128
SHORT = 2
SLIDES = 1
BLK_CAP = 7
WIDTH = 640
REPLICAS = 4
TILE_DEVS = 128
BLOCKS = 896


def layout_group(group_key):
    slot_total = TILE_DEVS * BLK_CAP
    positions = jnp.arange(slot_total, dtype=jnp.int32)
    live_count = jax.random.randint(jax.random.fold_in(group_key, 1), (TILE_DEVS,), BLK_CAP - SHORT, BLK_CAP + 1)
    shuffled = jax.random.permutation(jax.random.fold_in(group_key, 2), TILE_DEVS)
    live_count = live_count.at[shuffled[0]].set(BLK_CAP).at[shuffled[1]].set(BLK_CAP - SHORT)
    block_total = jnp.sum(live_count)
    cut_score = jax.random.randint(jax.random.fold_in(group_key, 3), (slot_total,), 0, 1 << 20) * slot_total + positions
    cut_score = jnp.where((positions >= 1) & (positions < block_total), cut_score, -1 - positions)
    ranked = jnp.argsort(-cut_score)
    cut_points = jnp.sort(ranked[:SLIDES - 1]).astype(jnp.int32)
    bounds = jnp.concatenate([jnp.zeros((1,), jnp.int32), cut_points, block_total[None].astype(jnp.int32)])
    blocks_of = bounds[1:] - bounds[:-1]
    slide_of = jnp.sum((positions[:, None] >= cut_points[None, :]).astype(jnp.int32), axis=1)
    rank_of = positions - bounds[slide_of]
    short_rows = jax.random.randint(jax.random.fold_in(group_key, 4), (SLIDES,), 0, TILE_ROWS)
    counts = blocks_of * TILE_ROWS - short_rows
    shuffle_score = jax.random.randint(jax.random.fold_in(group_key, 5), (slot_total,), 0, 1 << 20) * slot_total + positions
    shuffle_score = jnp.where(positions < block_total, shuffle_score, (1 << 30) + positions)
    placement = jnp.argsort(shuffle_score).astype(jnp.int32)
    offset = jnp.cumsum(live_count) - live_count
    slot_ids = jnp.arange(BLK_CAP, dtype=jnp.int32)
    linear = offset[:, None] + slot_ids[None, :]
    occupied = slot_ids[None, :] < live_count[:, None]
    chosen_block = placement[jnp.where(occupied, linear, 0)]
    slides = jnp.where(occupied, slide_of[chosen_block], -1).reshape(-1).astype(jnp.int32)
    ranks = jnp.where(occupied, rank_of[chosen_block], 0).reshape(-1).astype(jnp.int32)
    return (slides, ranks, counts.astype(jnp.int32))


def layout_all(key):
    base_key = jax.random.fold_in(key, 11)
    group_keys = jax.vmap(lambda group_id: jax.random.fold_in(base_key, group_id))(jnp.arange(REPLICAS))
    return jax.vmap(layout_group)(group_keys)


def draw_block_slide(key, part):
    return layout_all(key)[0]


def draw_block_rank(key, part):
    return layout_all(key)[1]


def draw_tile_count(key, part):
    return layout_all(key)[2]


def embed_block(key, group_id, block_id):
    block_key = jax.random.fold_in(jax.random.fold_in(jax.random.fold_in(key, 101), group_id), block_id)
    return jnp.clip(jax.random.normal(block_key, (TILE_ROWS, D_IN), jnp.float32), -6.0, 6.0)


def key_weight(key):
    drawn = jax.random.normal(jax.random.fold_in(key, 109), (D_IN, WIDTH), jnp.float32) / math.sqrt(D_IN)
    return jnp.clip(drawn, -0.2, 0.2)


def draw_tile_embed(key, part):
    block_ids = jnp.arange(BLOCKS, dtype=jnp.int32)

    def per_group(group_id):

        def per_block(block_id):
            return embed_block(key, group_id, block_id)
        return jax.vmap(per_block)(block_ids)
    table = jax.vmap(per_group)(jnp.arange(REPLICAS, dtype=jnp.int32))
    return jnp.clip(table, -24.0, 24.0).astype(jnp.bfloat16)


def draw_w_key(key, part):
    return key_weight(key).astype(jnp.bfloat16)


def draw_queries(key, part):
    drawn = 3.0 * jnp.clip(jax.random.normal(jax.random.fold_in(key, 111), (LATENTS, WIDTH), jnp.float32), -6.0, 6.0)
    return jnp.clip(drawn, -160.0, 160.0).astype(jnp.bfloat16)


def levels(key, dims, split, smallest, high):
    def one(position, blocks):
        draws = jax.random.uniform(jax.random.fold_in(jax.random.fold_in(key, 6), position), (blocks,), jnp.float32, smallest / len(split), high / len(split))
        return jnp.repeat(jnp.exp(draws), dims[position] // blocks).reshape((-1,) + (1,) * (len(dims) - position - 1))

    gain = one(*split[0])
    for cut in split[1:]:
        gain = gain * one(*cut)
    return gain


def noise(stream_key, extent, deviation, reach, pieces=(), kind=jnp.bfloat16):
    loudness = levels(stream_key, extent, pieces, -0.22, 0.18) if pieces else 1.0
    values = jax.random.normal(stream_key, extent, jnp.float32) * deviation * loudness
    return jnp.minimum(jnp.maximum(values, -reach), reach).astype(kind)


def setup_inputs(seed: int = 0) -> dict:
    key_of = jax.random.split(jax.random.key(seed), 9)
    return {
        "tile_embed": draw_tile_embed(jax.random.fold_in(key_of[8], 71), 0),
        "block_slide": draw_block_slide(jax.random.fold_in(key_of[8], 71), 0),
        "block_rank": draw_block_rank(jax.random.fold_in(key_of[8], 71), 0),
        "tile_count": draw_tile_count(jax.random.fold_in(key_of[8], 71), 0),
        "queries": draw_queries(jax.random.fold_in(key_of[8], 71), 0),
        "w_key": draw_w_key(jax.random.fold_in(key_of[8], 71), 0),
        "w_value": noise(key_of[6], (D_IN, WIDTH), D_IN ** -0.5, 0.15625, ((0, 4),)),
        "d_attended": noise(key_of[7], (REPLICAS, SLIDES, LATENTS, WIDTH), 1.0, 6.0, ((0, 4),)),
    }


MASKED_SCORE = -1e+30

def round_half(values):
    return lax.optimization_barrier(values.astype(jnp.bfloat16)).astype(jnp.float32)

def widen_heads(values):
    return jnp.repeat(values, HEAD_DIM, axis=-1)

def masked_scores(query_heads, key_part, slide_id, block_place, counts, score_scale):
    row_count = key_part.shape[0]
    key_heads = key_part.astype(jnp.float32).reshape(row_count, HEADS, HEAD_DIM)
    scores = jnp.einsum('ihe,the->hit', query_heads, key_heads) * score_scale
    limit = counts[jnp.maximum(slide_id, 0)]
    row_index = jnp.arange(row_count, dtype=jnp.int32)
    live_rows = (block_place * row_count + row_index < limit) & (slide_id >= 0)
    return jnp.where(live_rows[None, None, :], scores, MASKED_SCORE)

def group_pass(embeds, slides, ranks, counts, queries, w_both, d_out):
    slide_count = counts.shape[0]
    latent_count = queries.shape[0]
    feature_width = queries.shape[1]
    score_scale = 1.0 / math.sqrt(HEAD_DIM)
    query_heads = queries.astype(jnp.float32).reshape(latent_count, HEADS, HEAD_DIM)
    slide_index = jnp.arange(slide_count, dtype=jnp.int32)

    def forward(carry, item):
        maxima, totals, summed = carry
        block_rows, slide_id, block_place = item
        projected = jnp.dot(block_rows, w_both, preferred_element_type=jnp.float32).astype(jnp.bfloat16)
        scores = masked_scores(query_heads, projected[:, :feature_width], slide_id, block_place, counts, score_scale)
        block_max = lax.optimization_barrier(jnp.max(scores, axis=2))
        weights = jnp.exp(scores - block_max[:, :, None])
        block_total = lax.optimization_barrier(jnp.sum(weights, axis=2)).T
        value_heads = projected[:, feature_width:].astype(jnp.float32).reshape(-1, HEADS, HEAD_DIM)
        block_out = jnp.einsum('hit,the->ihe', round_half(weights), value_heads).reshape(latent_count, feature_width)
        chosen = (slide_index == slide_id)[:, None, None]
        new_max = jnp.where(chosen, jnp.maximum(maxima, block_max.T[None]), maxima)
        retain = jnp.exp(maxima - new_max)
        admit = jnp.where(chosen, jnp.exp(block_max.T[None] - new_max), 0.0)
        totals = retain * totals + admit * block_total[None]
        summed = widen_heads(retain) * summed + widen_heads(admit) * block_out[None]
        return ((new_max, totals, summed), projected)
    start_state = (jnp.full((slide_count, latent_count, HEADS), MASKED_SCORE, jnp.float32), jnp.zeros((slide_count, latent_count, HEADS), jnp.float32), jnp.zeros((slide_count, latent_count, feature_width), jnp.float32))
    (maxima, totals, summed), stored = lax.scan(forward, start_state, (embeds, slides, ranks))
    attended = (summed / widen_heads(totals)).astype(jnp.bfloat16)
    log_total = maxima + jnp.log(totals)
    products = d_out.astype(jnp.float32) * attended.astype(jnp.float32)
    row_delta = lax.optimization_barrier(jnp.sum(products.reshape(slide_count, latent_count, HEADS, HEAD_DIM), axis=3))

    def backward(carry, item):
        projected, slide_id, block_place = item
        safe_slide = jnp.maximum(slide_id, 0)
        scores = masked_scores(query_heads, projected[:, :feature_width], slide_id, block_place, counts, score_scale)
        probabilities = jnp.exp(scores - log_total[safe_slide].T[:, :, None])
        slide_grad = d_out[safe_slide].astype(jnp.float32).reshape(latent_count, HEADS, HEAD_DIM)
        value_heads = projected[:, feature_width:].astype(jnp.float32).reshape(-1, HEADS, HEAD_DIM)
        value_rows = jnp.einsum('hit,ihe->the', round_half(probabilities), slide_grad).astype(jnp.bfloat16)
        prob_grad = jnp.einsum('ihe,the->hit', slide_grad, value_heads)
        score_grad = round_half(probabilities * (prob_grad - row_delta[safe_slide].T[:, :, None]) * score_scale)
        key_rows = jnp.einsum('hit,ihe->the', score_grad, query_heads).astype(jnp.bfloat16)
        joined = jnp.concatenate([key_rows.reshape(-1, feature_width), value_rows.reshape(-1, feature_width)], axis=1)
        return (carry, joined)
    unused, grads = lax.scan(backward, jnp.int32(0), (stored, slides, ranks))
    flat_embed = embeds.reshape(-1, embeds.shape[-1])
    flat_grads = grads.reshape(-1, 2 * feature_width)
    weight_grad = jnp.dot(flat_embed.T, flat_grads, preferred_element_type=jnp.float32)
    return (attended, weight_grad)

def reference(tile_embed, block_slide, block_rank, tile_count, queries, w_key, w_value, d_attended):
    w_both = jnp.concatenate([w_key, w_value], axis=1)
    feature_width = w_key.shape[1]
    outputs = []
    grad_total = jnp.zeros((w_key.shape[0], 2 * feature_width), jnp.float32)
    for group_id in range(REPLICAS):
        attended, weight_grad = group_pass(tile_embed[group_id], block_slide[group_id], block_rank[group_id], tile_count[group_id], queries, w_both, d_attended[group_id])
        outputs.append(attended)
        grad_total = grad_total + weight_grad
    return (jnp.stack(outputs), grad_total[:, :feature_width], grad_total[:, feature_width:])
```

```python
import jax
import jax.numpy as jnp
from jax import lax
from jax.experimental import pallas as pl
from jax.experimental.pallas import tpu as pltpu
from jax.sharding import Mesh, PartitionSpec as P

HEAD_DIM = 64
OWN_HEADS = 5
HALF = OWN_HEADS * HEAD_DIM
LANES = 128
SCORE_SCALE = 0.125
MASKED_SCORE = -1e30
TOTAL_LANE = HEAD_DIM
PEAK_LANE = HEAD_DIM + 1
DELTA_LANE = HEAD_DIM + 2

GRID = (8, 8, 2, 4)
AXES = ("z", "y", "c", "x")
TILES = ("z", "y", "c")

NT = (((1,), (1,)), ((), ()))
TN = (((0,), (0,)), ((), ()))
NN = (((1,), (0,)), ((), ()))


def mm(one, two, dims):
    return lax.dot_general(one, two, dims, preferred_element_type=jnp.float32)


def lane_of(shape):
    return lax.broadcasted_iota(jnp.int32, shape, len(shape) - 1)


def swap_halves(part):
    return jnp.concatenate([part[:, HEAD_DIM:], part[:, :HEAD_DIM]], axis=1)


def pair_diagonal(part):
    lane = lane_of(part.shape)
    zero = jnp.zeros_like(part)
    return jnp.concatenate([jnp.where(lane < HEAD_DIM, part, zero), jnp.where(lane < HEAD_DIM, zero, part)], axis=0)


def own_half(ref, first):
    full = ref[...].astype(jnp.float32)
    part = jnp.where(first, full[:, :HALF], full[:, HALF:])
    last = jnp.concatenate([part[:, 256:], jnp.zeros_like(part[:, 256:])], axis=1)
    return [piece.astype(jnp.bfloat16) for piece in (part[:, :128], part[:, 128:256], last)]


def query_sides(parts):
    return [pair_diagonal(parts[0]), pair_diagonal(parts[1]), parts[2]]


def value_sides(parts):
    return [pair_diagonal(parts[0]), pair_diagonal(parts[1]), swap_halves(parts[2])]


def key_value(block):
    middle = block[:, 256:384]
    return [(block[:, :128], block[:, 384:512]), (block[:, 128:256], block[:, 512:]), (middle, middle)]


def masked(scores, limit_ref, base, block_rows):
    pieces = []
    for block in range(scores.shape[0] // block_rows):
        piece = scores[block * block_rows : (block + 1) * block_rows] * SCORE_SCALE
        row = lax.broadcasted_iota(jnp.int32, piece.shape, 0)
        pieces.append(jnp.where(row < limit_ref[base + block], piece, MASKED_SCORE))
    return jnp.concatenate(pieces, axis=0)


def turn_kernel(source_ref, x_ref, out_ref):
    chosen = lane_of((out_ref.shape[0], x_ref.shape[1])) == source_ref[...]
    out_ref[...] = mm(jnp.where(chosen, 1.0, 0.0).astype(jnp.bfloat16), x_ref[...], NT).astype(jnp.bfloat16)


def forward_kernel(
    limit_ref, place_ref, x_ref, w0_ref, w1_ref, w2_ref, w3_ref, q_ref, after_ref, kv_ref, stat_ref, w_ref, *, block_rows
):
    step = pl.program_id(0)
    share = w0_ref.shape[0]

    @pl.when(step == 0)
    def _():
        for index, part in enumerate((w0_ref, w1_ref, w2_ref, w3_ref)[: w_ref.shape[0] // share]):
            start = pl.multiple_of(place_ref[1 + index] * share, share)
            w_ref[pl.ds(start, share), :] = part[...]

    kv = mm(x_ref[...], w_ref[...], NN).astype(jnp.bfloat16)
    kv_ref[...] = kv
    blocks = kv.shape[0] // block_rows
    heads = []
    for (keys, values), q_side in zip(key_value(kv), query_sides(own_half(q_ref, place_ref[0] == 0))):
        scores = masked(mm(keys, q_side, NT), limit_ref, step * blocks, block_rows)
        peak = jnp.max(scores, axis=0, keepdims=True)
        p = jnp.exp(scores - peak)
        total = jnp.sum(p, axis=0, keepdims=True)
        both = mm(p.astype(jnp.bfloat16), values, TN)
        pad = jnp.zeros((6, peak.shape[1]), jnp.float32)
        columns = jnp.concatenate([total, peak, pad], axis=0).T
        for half in range(peak.shape[1] // HEAD_DIM):
            rows = slice(half * HEAD_DIM, (half + 1) * HEAD_DIM)
            out = both[rows]
            if half == 1 or peak.shape[1] == HEAD_DIM:
                out = swap_halves(out)
            lane = lane_of(out.shape)
            out = jnp.where(lane < HEAD_DIM, out, jnp.where(lane == TOTAL_LANE, columns[rows, :1], columns[rows, 1:2]))
            heads.append(out)

    @pl.when(step == 0)
    def _():
        for head, out in enumerate(heads):
            stat_ref[:, head * LANES : (head + 1) * LANES] = out

    @pl.when(step != 0)
    def _():
        for head, out in enumerate(heads):
            had = stat_ref[:, head * LANES : (head + 1) * LANES]
            had_peak = had[:, PEAK_LANE : PEAK_LANE + 1]
            new_peak = out[:, PEAK_LANE : PEAK_LANE + 1]
            top = jnp.maximum(had_peak, new_peak)
            merged = had * jnp.exp(had_peak - top) + out * jnp.exp(new_peak - top)
            stat_ref[:, head * LANES : (head + 1) * LANES] = jnp.where(lane_of(out.shape) == PEAK_LANE, top, merged)


def combine_kernel(in_ref, out_ref, *, sources):
    for head in range(OWN_HEADS):
        cols = slice(head * LANES, (head + 1) * LANES)
        terms = in_ref[:, cols]
        if sources != terms.shape[0]:
            terms = terms.reshape(sources, -1, LANES)
        lane = lane_of(terms.shape)
        peak = jnp.max(jnp.where(lane == PEAK_LANE, terms, -jnp.inf), axis=-1, keepdims=True)
        top = jnp.max(peak, axis=0, keepdims=True)
        summed = jnp.sum(terms * jnp.exp(peak - top), axis=0, keepdims=True)
        lane = lane_of(summed.shape)
        total = jnp.sum(jnp.where(lane == TOTAL_LANE, summed, 0.0), axis=-1, keepdims=True)
        attended = (summed / total).astype(jnp.bfloat16).astype(jnp.float32)
        row = jnp.where(lane < HEAD_DIM, attended, jnp.where(lane == TOTAL_LANE, top + jnp.log(total), 0.0))
        out_ref[:, cols] = jnp.broadcast_to(row, terms.shape).reshape(out_ref.shape[0], LANES)


def backward_kernel(
    limit_ref, place_ref, xt_ref, kv_ref, q_ref, d_ref, merged_ref, attended_ref, grad_ref, rows_ref, *, block_rows
):
    @pl.when(pl.program_id(0) == 0)
    def _():
        first = place_ref[0] == 0
        d_parts = own_half(d_ref, first)
        q_sides = query_sides(own_half(q_ref, first))
        d_sides = value_sides(d_parts)
        d_heads = [d_parts[0], swap_halves(d_parts[0]), d_parts[1], swap_halves(d_parts[1]), d_parts[2]]
        heads = []
        for head in range(OWN_HEADS):
            block = merged_ref[:, head * LANES : (head + 1) * LANES]
            lane = lane_of(block.shape)
            product = jnp.where(lane < HEAD_DIM, block * d_heads[head].astype(jnp.float32), 0.0)
            delta = jnp.sum(product, axis=1, keepdims=True)
            heads.append(jnp.where(lane == DELTA_LANE, delta, block))
        lane = lane_of(heads[0].shape)
        for pair in range(2):
            both = jnp.where(lane < HEAD_DIM, heads[2 * pair], swap_halves(heads[2 * pair + 1]))
            attended_ref[:, pair * LANES : (pair + 1) * LANES] = both.astype(jnp.bfloat16)
        attended_ref[:, 256:] = heads[4].astype(jnp.bfloat16)
        turned = [jnp.concatenate(heads[:2], axis=0).T, jnp.concatenate(heads[2:4], axis=0).T, heads[4].T]
        half_rows = kv_ref.shape[0] // 2
        blocks = half_rows // block_rows

        @pl.loop(0, 2)
        def _(half):
            start = pl.multiple_of(half * half_rows, half_rows)
            kv = kv_ref[pl.ds(start, half_rows), :]
            rows = []
            for (keys, values), q_side, d_side, turn in zip(key_value(kv), q_sides, d_sides, turned):
                scores = masked(mm(keys, q_side, NT), limit_ref, half * blocks, block_rows)
                probs = jnp.exp(scores - turn[TOTAL_LANE : TOTAL_LANE + 1])
                prob_grad = mm(values, d_side, NT)
                score_grad = probs * (prob_grad - turn[DELTA_LANE : DELTA_LANE + 1]) * SCORE_SCALE
                rows.append((mm(score_grad.astype(jnp.bfloat16), q_side, NN), mm(probs.astype(jnp.bfloat16), d_side, NN)))
            parts = [rows[0][0], rows[1][0], rows[2][0] + rows[2][1], rows[0][1], rows[1][1]]
            for index, part in enumerate(parts):
                rows_ref[pl.ds(start, half_rows), index * LANES : (index + 1) * LANES] = part.astype(jnp.bfloat16)

    grad_ref[...] = mm(xt_ref[...], rows_ref[...], NN).astype(jnp.bfloat16)


def first_fold_kernel(in_ref, out_ref):
    pieces, padded, _ = out_ref.shape
    total = in_ref[0].astype(jnp.float32)
    for source in range(1, in_ref.shape[0]):
        total = total + in_ref[source].astype(jnp.float32)
    length = total.shape[0] // pieces
    for piece in range(pieces):
        part = total[piece * length : (piece + 1) * length]
        if padded != length:
            part = jnp.concatenate([part, jnp.zeros((padded - length, part.shape[1]), jnp.float32)], axis=0)
        out_ref[piece] = part.astype(jnp.bfloat16)


def second_fold_kernel(place_ref, in_ref, out_ref, *, length, reps):
    total = in_ref[0].astype(jnp.float32)
    for source in range(1, in_ref.shape[0]):
        total = total + in_ref[source].astype(jnp.float32)
    keys = total[:, :HALF]
    values = jnp.concatenate([total[:, 384:], total[:, HALF:384]], axis=1)
    _, padded, lanes = out_ref.shape
    width = 2 * HALF // reps
    out_ref[...] = jnp.zeros_like(out_ref)
    for core in range(2):
        rows = slice(core * length, (core + 1) * length)
        for local in range(reps // 2):
            cols = slice(local * width, (local + 1) * width)
            part = jnp.concatenate([keys[rows, cols], values[rows, cols]], axis=1)
            if lanes != part.shape[1]:
                part = jnp.concatenate([part, jnp.zeros((length, lanes - part.shape[1]), jnp.float32)], axis=1)
            if padded != length:
                part = jnp.concatenate([part, jnp.zeros((padded - length, lanes), jnp.float32)], axis=0)
            out_ref[core * reps + place_ref[0] * (reps // 2) + local] = part.astype(jnp.bfloat16)


def whole(shape):
    return pl.BlockSpec(shape, lambda step, *_: (0,) * len(shape))


def row_block(rows, cols):
    return pl.BlockSpec((rows, cols), lambda step, *_: (step, 0))


def shaped(shape, dtype=jnp.bfloat16):
    return jax.ShapeDtypeStruct(shape, dtype)


def call(kernel, name, scalars, grid, in_specs, out_specs, out_shape, flops, nbytes, scratch=()):
    return pl.pallas_call(
        kernel,
        name=name,
        out_shape=out_shape,
        grid_spec=pltpu.PrefetchScalarGridSpec(
            num_scalar_prefetch=scalars, grid=grid, in_specs=in_specs, out_specs=out_specs, scratch_shapes=scratch
        ),
        compiler_params=pltpu.CompilerParams(dimension_semantics=("arbitrary",)),
        cost_estimate=pl.CostEstimate(flops=flops, bytes_accessed=nbytes, transcendentals=0),
    )


def device(z, y, c, x):
    _, ys, cs, xs = GRID
    return ((z * ys + y) * cs + c) * xs + x


def line_groups(along):
    zs, ys, _, xs = GRID
    groups = []
    for core in range(2):
        for x in range(xs):
            if along[core] == "z":
                groups += [[device(z, y, core, x) for z in range(zs)] for y in range(ys)]
            else:
                groups += [[device(z, y, core, x) for y in range(ys)] for z in range(zs)]
    return groups


def padded16(count):
    return -(-count // 16) * 16


def body(tile_embed, block_slide, block_rank, tile_count, queries, w_key, w_value, d_attended):
    zs, ys, _, xs = GRID
    _, slots, block_rows, width_in = tile_embed.shape
    rows = slots * block_rows
    latents, width = queries.shape
    core = lax.axis_index("c")
    rep = lax.axis_index("x")
    first = core == 0
    both_rows = 2 * rows
    big_flops = 2 * both_rows * width_in * width

    def partner(value):
        return lax.ppermute(value, "c", [(0, 1), (1, 0)])

    x_own = tile_embed.reshape(rows, width_in)
    limits = jnp.where(block_slide[0] >= 0, tile_count[0, 0] - block_rank[0] * block_rows, 0)
    x_all = jnp.concatenate([x_own, partner(x_own)], axis=0)
    limits = jnp.concatenate([limits, partner(limits)])

    key_half = jnp.where(first, w_key[:, :HALF], w_key[:, HALF:])
    value_half = jnp.where(first, w_value[:, :HALF], w_value[:, HALF:])
    w_own = jnp.concatenate([key_half, value_half[:, 256:], value_half[:, :256]], axis=1)
    w_parts = [w_own]
    for hop in range(1, xs):
        w_parts.append(lax.ppermute(w_own, "x", [(x, (x + hop) % xs) for x in range(xs)]))
    origin = [(rep - hop) % xs for hop in range(4)]
    place = jnp.stack([core, *origin]).astype(jnp.int32)
    w_parts = (w_parts + [w_own] * 4)[:4]

    unit = width_in // (zs * ys)
    natural = jnp.arange(width_in, dtype=jnp.int32)
    by_y = natural.reshape(zs, ys, unit).transpose(1, 0, 2).reshape(width_in)
    source = jnp.where(first, natural, by_y)[:, None]
    turned = call(
        turn_kernel, "turn", 0, (5,), [row_block(width_in // 5, 1), whole(x_all.shape)],
        row_block(width_in // 5, both_rows), shaped((width_in, both_rows)),
        2 * both_rows * width_in * width_in, 9 << 20,
    )(source, x_all)

    kv, stats = call(
        lambda *refs: forward_kernel(*refs, block_rows=block_rows), "forward_pass", 2, (2,),
        [row_block(rows, width_in), *[whole(w_own.shape)] * 4, whole(queries.shape), pl.BlockSpec(memory_space=pl.ANY)],
        (row_block(rows, width), whole((latents, OWN_HEADS * LANES))),
        (shaped((both_rows, width)), shaped((latents, OWN_HEADS * LANES), jnp.float32)),
        big_flops, 10 << 20, [pltpu.VMEM((width_in, width), jnp.bfloat16)],
    )(limits, place, x_all, *w_parts, queries, turned)

    chips = ("z", "y")
    stats = lax.all_to_all(stats, chips, 0, 0, tiled=True)
    merged = call(
        lambda *refs: combine_kernel(*refs, sources=zs * ys), "combine", 0, (1,),
        [whole(stats.shape)], whole(stats.shape), shaped(stats.shape, jnp.float32), stats.size * 4, stats.size * 8,
    )(stats)
    merged = lax.all_to_all(merged, chips, 0, 0, tiled=True)

    d_out = d_attended.reshape(latents, width)
    attended, grads = call(
        lambda *refs: backward_kernel(*refs, block_rows=block_rows), "backward_pass", 2, (2,),
        [row_block(width_in // 2, both_rows), whole(kv.shape), whole(queries.shape), whole(d_out.shape), whole(merged.shape)],
        (whole((latents, 3 * LANES)), row_block(width_in // 2, width)),
        (shaped((latents, 3 * LANES)), shaped((width_in, width))),
        big_flops, 10 << 20, [pltpu.VMEM((both_rows, width), jnp.bfloat16)],
    )(limits, place, turned, kv, queries, d_out, merged)
    mine = attended[:, :HALF]
    theirs = partner(mine)
    attended = jnp.where(first, jnp.concatenate([mine, theirs], axis=1), jnp.concatenate([theirs, mine], axis=1))

    received = lax.all_to_all(grads, AXES, 0, 0, axis_index_groups=line_groups("zy"), tiled=True)
    received = received.reshape(zs, width_in // zs, width)
    chunk = (ys, padded16(unit), width)
    pieces = call(
        first_fold_kernel, "first_fold", 0, (1,), [whole(received.shape)], whole(chunk), shaped(chunk),
        received.size, received.size * 2,
    )(received)
    received = lax.all_to_all(pieces, AXES, 0, 0, axis_index_groups=line_groups("yz"), tiled=True)
    chunk = (2 * xs, padded16(unit // 2), -(-2 * width // xs // LANES) * LANES)
    pieces = call(
        lambda *refs: second_fold_kernel(*refs, length=unit // 2, reps=xs), "second_fold", 1, (1,),
        [whole(received.shape)], whole(chunk), shaped(chunk), received.size, received.size * 2,
    )(place, received)
    received = lax.all_to_all(pieces, ("c", "x"), 0, 0, tiled=True)
    final = jnp.sum(received.astype(jnp.float32), axis=0)[: unit // 2]
    share = width // xs
    return (attended.reshape(1, 1, latents, width), final[:, :share], final[:, share : 2 * share])


def solution(mesh):
    grid = Mesh(mesh.devices.reshape(GRID), AXES)
    placed = (
        P("x", TILES, None, None),
        P("x", TILES),
        P("x", TILES),
        P("x", None),
        P(),
        P("x", None),
        P("x", None),
        P("x", None, None, None),
    )
    return jax.shard_map(
        body,
        mesh=grid,
        in_specs=placed,
        out_specs=(P("x", None, None, None), P(TILES, "x"), P(TILES, "x")),
        check_vma=False,
    )
```

```python
import jax
import jax.numpy as jnp
from jax import lax
from jax.experimental import pallas as pl
from jax.experimental.pallas import tpu as pltpu
from jax.sharding import Mesh, PartitionSpec as P

HEAD_DIM = 64
OWN_HEADS = 5
HALF = OWN_HEADS * HEAD_DIM
LANES = 128
SCORE_SCALE = 0.125
MASKED_SCORE = -1e30
TOTAL_LANE = HEAD_DIM
PEAK_LANE = HEAD_DIM + 1
DELTA_LANE = HEAD_DIM + 2

GRID = (8, 8, 2, 4)
AXES = ("z", "y", "c", "x")
TILES = ("z", "y", "c")

NT = (((1,), (1,)), ((), ()))
TN = (((0,), (0,)), ((), ()))
NN = (((1,), (0,)), ((), ()))


def mm(one, two, dims):
    return lax.dot_general(one, two, dims, preferred_element_type=jnp.float32)


def lane_of(shape):
    return lax.broadcasted_iota(jnp.int32, shape, len(shape) - 1)


def swap_halves(part):
    return jnp.concatenate([part[:, HEAD_DIM:], part[:, :HEAD_DIM]], axis=1)


def pair_diagonal(part):
    lane = lane_of(part.shape)
    zero = jnp.zeros_like(part)
    return jnp.concatenate([jnp.where(lane < HEAD_DIM, part, zero), jnp.where(lane < HEAD_DIM, zero, part)], axis=0)


def own_half(ref, first, scale=1.0):
    full = ref[...].astype(jnp.float32) * scale
    part = jnp.where(first, full[:, :HALF], full[:, HALF:])
    last = jnp.concatenate([part[:, 256:], jnp.zeros_like(part[:, 256:])], axis=1)
    return [piece.astype(jnp.bfloat16) for piece in (part[:, :128], part[:, 128:256], last)]


def diagonal(one, two):
    right = jnp.zeros((one.shape[0], two.shape[1]), one.dtype)
    below = jnp.zeros((two.shape[0], one.shape[1]), one.dtype)
    return jnp.concatenate([jnp.concatenate([one, right], axis=1), jnp.concatenate([below, two], axis=1)], axis=0)


def masked(scores, limit_ref, block_rows):
    pieces = []
    for block in range(scores.shape[0] // block_rows):
        piece = scores[block * block_rows : (block + 1) * block_rows]
        row = lax.broadcasted_iota(jnp.int32, piece.shape, 0)
        pieces.append(jnp.where(row < limit_ref[block], piece, MASKED_SCORE))
    return jnp.concatenate(pieces, axis=0)


def turn_kernel(core_ref, x_ref, out_ref, *, zs, ys):
    rows, unit = out_ref.shape[0], x_ref.shape[1] // (zs * ys)
    row = lax.broadcasted_iota(jnp.int32, (rows, 1), 0) + pl.program_id(0) * rows
    middle = row.astype(jnp.float32) + 0.5
    outer = (middle * (1.0 / (zs * unit))).astype(jnp.int32)
    piece = (middle * (1.0 / unit)).astype(jnp.int32)
    by_y = ((piece - outer * zs) * ys + outer) * unit + row - piece * unit
    source = jnp.where(core_ref[0] == 0, row, by_y)
    chosen = lane_of((rows, x_ref.shape[1])) == source
    out_ref[...] = mm(jnp.where(chosen, 1.0, 0.0).astype(jnp.bfloat16), x_ref[...], NT).astype(jnp.bfloat16)


def forward_kernel(core_ref, rep_ref, limit_ref, limit2_ref, xo_ref, xp_ref, *refs, block_rows, reps):
    part_refs = refs[:reps]
    q_ref, kv_ref, stat_ref, w_ref, x_ref, both_ref, x_sem, w_sem = refs[reps:]
    step = pl.program_id(0)
    share = part_refs[0].shape[0]
    blocks = x_ref.shape[1] // block_rows

    def tiles(half):
        return pltpu.make_async_copy((xo_ref, xp_ref)[half], x_ref.at[half], x_sem.at[half])

    def weights(hop):
        start = pl.multiple_of(((rep_ref[0] + reps - hop) % reps) * share, share)
        return pltpu.make_async_copy(part_refs[hop], w_ref.at[pl.ds(start, share), :], w_sem.at[hop])

    @pl.when(step == 0)
    def _():
        tiles(0).start()
        for hop in range(reps):
            weights(hop).start()
        tiles(1).start()
        for block in range(blocks):
            both_ref[block] = limit_ref[block]
            both_ref[blocks + block] = limit2_ref[block]
        tiles(0).wait()
        for hop in range(reps):
            weights(hop).wait()

    @pl.when(step != 0)
    def _():
        tiles(1).wait()

    kv = mm(x_ref[step], w_ref[...], NN).astype(jnp.bfloat16)
    kv_ref[...] = kv
    q_parts = own_half(q_ref, core_ref[0] == 0, SCORE_SCALE)
    wide = diagonal(pair_diagonal(q_parts[0]), pair_diagonal(q_parts[1]))
    middle = kv[:, 256:384]
    heads = []
    for keys, q_side, values in (
        (kv[:, :256], wide, (kv[:, 384:512], kv[:, 512:])),
        (middle, q_parts[2], (middle,)),
    ):
        scores = masked(mm(keys, q_side, NT), both_ref.at[pl.ds(step * blocks, blocks)], block_rows)
        peak = jnp.max(scores, axis=0, keepdims=True)
        p = jnp.exp(scores - peak)
        total = jnp.sum(p, axis=0, keepdims=True)
        pad = jnp.zeros((6, peak.shape[1]), jnp.float32)
        columns = jnp.concatenate([total, peak, pad], axis=0).T
        p = p.astype(jnp.bfloat16)
        for index, value in enumerate(values):
            span = min(LANES, p.shape[1])
            both = mm(p[:, index * span : (index + 1) * span], value, TN)
            for half in range(span // HEAD_DIM):
                rows = slice(half * HEAD_DIM, (half + 1) * HEAD_DIM)
                stat = columns[index * span + half * HEAD_DIM : index * span + (half + 1) * HEAD_DIM]
                out = both[rows]
                if half == 1 or span == HEAD_DIM:
                    out = swap_halves(out)
                lane = lane_of(out.shape)
                heads.append(
                    jnp.where(lane < HEAD_DIM, out, jnp.where(lane == TOTAL_LANE, stat[:, :1], stat[:, 1:2]))
                )

    @pl.when(step == 0)
    def _():
        for head, out in enumerate(heads):
            stat_ref[:, head, :] = out

    @pl.when(step != 0)
    def _():
        for head, out in enumerate(heads):
            had = stat_ref[:, head, :]
            had_peak = had[:, PEAK_LANE : PEAK_LANE + 1]
            new_peak = out[:, PEAK_LANE : PEAK_LANE + 1]
            top = jnp.maximum(had_peak, new_peak)
            merged = had * jnp.exp(had_peak - top) + out * jnp.exp(new_peak - top)
            stat_ref[:, head, :] = jnp.where(lane_of(out.shape) == PEAK_LANE, top, merged)


def combine_kernel(in_ref, out_ref, *, sources):
    terms = in_ref[...].reshape(sources, -1, OWN_HEADS, LANES)
    lane = lane_of(terms.shape)
    peak = jnp.max(jnp.where(lane == PEAK_LANE, terms, -jnp.inf), axis=-1, keepdims=True)
    top = jnp.max(peak, axis=0, keepdims=True)
    summed = jnp.sum(terms * jnp.exp(peak - top), axis=0, keepdims=True)
    lane = lane_of(summed.shape)
    total = jnp.sum(jnp.where(lane == TOTAL_LANE, summed, 0.0), axis=-1, keepdims=True)
    attended = (summed / total).astype(jnp.bfloat16).astype(jnp.float32)
    row = jnp.where(lane < HEAD_DIM, attended, jnp.where(lane == TOTAL_LANE, top + jnp.log(total), 0.0))
    out_ref[...] = jnp.broadcast_to(row, terms.shape).reshape(out_ref.shape)


def backward_kernel(
    core_ref, limit_ref, limit2_ref, to_ref, tp_ref, kv_ref, q_ref, d_ref, merged_ref, attended_ref, grad_ref,
    rows_ref, both_ref, *, block_rows,
):
    half_rows = kv_ref.shape[0] // 2

    @pl.when(pl.program_id(0) == 0)
    def _():
        first = core_ref[0] == 0
        d_parts = own_half(d_ref, first)
        q_parts = own_half(q_ref, first, SCORE_SCALE)
        sides = [diagonal(pair_diagonal(q_parts[pair]), pair_diagonal(d_parts[pair])) for pair in range(2)]
        last = jnp.concatenate([q_parts[2], swap_halves(d_parts[2])], axis=0)
        d_heads = [d_parts[0], swap_halves(d_parts[0]), d_parts[1], swap_halves(d_parts[1]), d_parts[2]]
        heads = []
        for head in range(OWN_HEADS):
            block = merged_ref[:, head, :]
            lane = lane_of(block.shape)
            product = jnp.where(lane < HEAD_DIM, block * d_heads[head].astype(jnp.float32), 0.0)
            delta = jnp.sum(product, axis=1, keepdims=True)
            heads.append(jnp.where(lane == DELTA_LANE, delta, block))
        lane = lane_of(heads[0].shape)
        for pair in range(2):
            both = jnp.where(lane < HEAD_DIM, heads[2 * pair], swap_halves(heads[2 * pair + 1]))
            attended_ref[:, pair * LANES : (pair + 1) * LANES] = both.astype(jnp.bfloat16)
        attended_ref[:, 256:] = heads[4].astype(jnp.bfloat16)
        turned = [jnp.concatenate(heads[:2], axis=0).T, jnp.concatenate(heads[2:4], axis=0).T, heads[4].T]
        blocks = half_rows // block_rows
        for block in range(blocks):
            both_ref[block] = limit_ref[block]
            both_ref[blocks + block] = limit2_ref[block]

        @pl.loop(0, 2)
        def _(half):
            start = pl.multiple_of(half * half_rows, half_rows)
            kv = kv_ref[pl.ds(start, half_rows), :]
            pairs = [
                jnp.concatenate([kv[:, :128], kv[:, 384:512]], axis=1),
                jnp.concatenate([kv[:, 128:256], kv[:, 512:]], axis=1),
                kv[:, 256:384],
            ]
            for index, (pair, side, turn) in enumerate(zip(pairs, [*sides, last], turned)):
                span = turn.shape[1]
                both = mm(pair, side, NT)
                scores = masked(both[:, :span], both_ref.at[pl.ds(half * blocks, blocks)], block_rows)
                probs = jnp.exp(scores - turn[TOTAL_LANE : TOTAL_LANE + 1])
                score_grad = probs * (both[:, span:] - turn[DELTA_LANE : DELTA_LANE + 1])
                pair = jnp.concatenate([score_grad.astype(jnp.bfloat16), probs.astype(jnp.bfloat16)], axis=1)
                rows = mm(pair, side, NN).astype(jnp.bfloat16)
                if index == 2:
                    rows_ref[pl.ds(start, half_rows), 256:384] = rows
                else:
                    rows_ref[pl.ds(start, half_rows), index * LANES : (index + 1) * LANES] = rows[:, :LANES]
                    rows_ref[pl.ds(start, half_rows), 384 + index * LANES : 512 + index * LANES] = rows[:, LANES:]

    grads = mm(to_ref[...], rows_ref[:half_rows, :], NN) + mm(tp_ref[...], rows_ref[half_rows:, :], NN)
    grad_ref[...] = grads.astype(jnp.bfloat16)


def fold_kernel(in_ref, out_ref, *, length, reps):
    total = in_ref[0].astype(jnp.float32)
    for source in range(1, in_ref.shape[0]):
        total = total + in_ref[source].astype(jnp.float32)
    keys = total[:, :HALF]
    values = jnp.concatenate([total[:, 384:], total[:, HALF:384]], axis=1)
    pieces, padded, lanes = out_ref.shape
    width = 2 * HALF // reps
    for local in range(reps // 2):
        cols = slice(local * width, (local + 1) * width)
        part = jnp.concatenate([keys[:, cols], values[:, cols]], axis=1)
        if lanes != part.shape[1]:
            part = jnp.concatenate([part, jnp.zeros((part.shape[0], lanes - part.shape[1]), jnp.float32)], axis=1)
        for block in range(2 * pieces // reps):
            piece = part[block * length : (block + 1) * length]
            if padded != length:
                piece = jnp.concatenate([piece, jnp.zeros((padded - length, lanes), jnp.float32)], axis=0)
            out_ref[block * (reps // 2) + local] = piece.astype(jnp.bfloat16)


def whole(shape):
    return pl.BlockSpec(shape, lambda step, *_: (0,) * len(shape))


def row_block(rows, cols):
    return pl.BlockSpec((rows, cols), lambda step, *_: (step, 0))


def shaped(shape, dtype=jnp.bfloat16):
    return jax.ShapeDtypeStruct(shape, dtype)


def call(kernel, name, scalars, grid, in_specs, out_specs, out_shape, flops, nbytes, scratch=()):
    return pl.pallas_call(
        kernel,
        name=name,
        out_shape=out_shape,
        grid_spec=pltpu.PrefetchScalarGridSpec(
            num_scalar_prefetch=scalars, grid=grid, in_specs=in_specs, out_specs=out_specs, scratch_shapes=scratch
        ),
        compiler_params=pltpu.CompilerParams(dimension_semantics=("arbitrary",)),
        cost_estimate=pl.CostEstimate(flops=flops, bytes_accessed=nbytes, transcendentals=0),
    )


def device(z, y, c, x):
    _, ys, cs, xs = GRID
    return ((z * ys + y) * cs + c) * xs + x


def first_groups():
    zs, ys, _, xs = GRID
    groups = []
    for x in range(xs):
        groups += [[device(z, y, 0, x) for z in range(zs)] for y in range(ys)]
        groups += [[device(z, y, 1, x) for y in range(ys)] for z in range(zs)]
    return groups


def second_groups():
    zs, ys, _, xs = GRID
    groups = [[device(z, y, 0, x) for y in range(ys) for x in range(xs)] for z in range(zs)]
    groups += [[device(z, y, 1, x) for z in range(zs) for x in range(xs)] for y in range(ys)]
    return groups


def padded_to(count, unit):
    return -(-count // unit) * unit


def body(tile_embed, block_slide, block_rank, tile_count, queries, w_key, w_value, d_attended):
    zs, ys, _, xs = GRID
    _, slots, block_rows, width_in = tile_embed.shape
    rows = slots * block_rows
    latents, width = queries.shape
    core = lax.axis_index("c")
    first = core == 0
    both_rows = 2 * rows
    big_flops = 2 * both_rows * width_in * width
    core_arg = core.astype(jnp.int32)[None]
    rep_arg = lax.axis_index("x").astype(jnp.int32)[None]
    anywhere = pl.BlockSpec(memory_space=pl.ANY)

    def partner(value):
        return lax.ppermute(value, "c", [(0, 1), (1, 0)])

    key_half = jnp.where(first, w_key[:, :HALF], w_key[:, HALF:])
    value_half = jnp.where(first, w_value[:, :HALF], w_value[:, HALF:])
    w_own = jnp.concatenate([key_half, value_half[:, 256:], value_half[:, :256]], axis=1)
    w_parts = [w_own]
    for hop in range(1, xs):
        w_parts.append(lax.ppermute(w_own, "x", [(x, (x + hop) % xs) for x in range(xs)]))

    x_own = tile_embed.reshape(rows, width_in)
    x_part = partner(x_own)
    limits = jnp.where(block_slide[0] >= 0, tile_count[0, 0] - block_rank[0] * block_rows, 0)
    limits2 = partner(limits)

    def turned(tiles, name):
        return call(
            lambda *refs: turn_kernel(*refs, zs=zs, ys=ys), name, 1, (5,), [whole(tiles.shape)],
            row_block(width_in // 5, rows), shaped((width_in, rows)), 2 * rows * width_in * width_in, 5 << 20,
        )(core_arg, tiles)

    turned_own = turned(x_own, "turn_own")
    turned_part = turned(x_part, "turn_partner")

    stat_shape = (latents, OWN_HEADS, LANES)
    scratch = [
        pltpu.VMEM((width_in, width), jnp.bfloat16),
        pltpu.VMEM((2, rows, width_in), jnp.bfloat16),
        pltpu.SMEM((2 * slots,), jnp.int32),
        pltpu.SemaphoreType.DMA((2,)),
        pltpu.SemaphoreType.DMA((xs,)),
    ]
    kv, stats = call(
        lambda *refs: forward_kernel(*refs[: 6 + xs], *refs[8 + xs :], block_rows=block_rows, reps=xs), "forward_pass", 4, (2,),
        [*[anywhere] * (4 + xs), whole(queries.shape)],
        (row_block(rows, width), whole(stat_shape)),
        (shaped((both_rows, width)), shaped(stat_shape, jnp.float32)), big_flops, 10 << 20, scratch,
    )(core_arg, rep_arg, limits, limits2, x_own, x_part, *w_parts, turned_own, turned_part, queries)

    chips = ("z", "y")
    stats = lax.all_to_all(stats, chips, 0, 0, tiled=True)
    merged = call(
        lambda *refs: combine_kernel(*refs, sources=zs * ys), "combine", 0, (1,),
        [whole(stat_shape)], whole(stat_shape), shaped(stat_shape, jnp.float32), stats.size * 4, stats.size * 8,
    )(stats)
    merged = lax.all_to_all(merged, chips, 0, 0, tiled=True)

    d_out = d_attended.reshape(latents, width)
    attended, grads = call(
        lambda *refs: backward_kernel(*refs, block_rows=block_rows), "backward_pass", 3, (2,),
        [
            row_block(width_in // 2, rows), row_block(width_in // 2, rows), whole(kv.shape), whole(queries.shape),
            whole(d_out.shape), whole(stat_shape),
        ],
        (whole((latents, 3 * LANES)), row_block(width_in // 2, width)),
        (shaped((latents, 3 * LANES)), shaped((width_in, width))),
        big_flops, 10 << 20, [pltpu.VMEM((both_rows, width), jnp.bfloat16), pltpu.SMEM((2 * slots,), jnp.int32)],
    )(core_arg, limits, limits2, turned_own, turned_part, kv, queries, d_out, merged)
    mine = attended[:, :HALF]
    theirs = partner(mine)
    attended = jnp.where(first, jnp.concatenate([mine, theirs], axis=1), jnp.concatenate([theirs, mine], axis=1))

    received = lax.all_to_all(grads, AXES, 0, 0, axis_index_groups=first_groups(), tiled=True)
    received = received.reshape(zs, width_in // zs, width)
    length = width_in // (2 * zs * ys)
    share = width // xs
    chunk = (ys * xs, padded_to(length, 16), padded_to(2 * share, LANES))
    pieces = call(
        lambda *refs: fold_kernel(*refs, length=length, reps=xs), "fold", 0, (1,), [whole(received.shape)],
        whole(chunk), shaped(chunk), received.size, received.size * 2,
    )(received)
    received = lax.all_to_all(pieces, AXES, 0, 0, axis_index_groups=second_groups(), tiled=True)
    total = jnp.sum(received.astype(jnp.float32), axis=0)[:length, : 2 * share]
    half = xs // 2
    home = [(c * xs + x, (x // half) * xs + c * half + x % half) for c in range(2) for x in range(xs)]
    total = lax.ppermute(total, ("c", "x"), home)
    return (attended.reshape(1, 1, latents, width), total[:, :share], total[:, share:])


def solution(mesh):
    grid = Mesh(mesh.devices.reshape(GRID), AXES)
    placed = (
        P("x", TILES, None, None),
        P("x", TILES),
        P("x", TILES),
        P("x", None),
        P(),
        P("x", None),
        P("x", None),
        P("x", None, None, None),
    )
    return jax.shard_map(
        body,
        mesh=grid,
        in_specs=placed,
        out_specs=(P("x", None, None, None), P(TILES, "x"), P(TILES, "x")),
        check_vma=False,
    )
```

```python
import jax
import jax.numpy as jnp
from jax import lax
from jax.experimental import pallas as pl
from jax.experimental.pallas import tpu as pltpu
from jax.sharding import Mesh, PartitionSpec as P

HEAD_DIM = 64
OWN_HEADS = 5
HALF = OWN_HEADS * HEAD_DIM
LANES = 128
SCORE_SCALE = 0.125
MASKED_SCORE = -1e30

VMEM_LIMIT = 32 << 20

GRID = (8, 8, 2, 4)
AXES = ("z", "y", "c", "x")
TILES = ("z", "y", "c")

NT = (((1,), (1,)), ((), ()))
TN = (((0,), (0,)), ((), ()))
NN = (((1,), (0,)), ((), ()))


def mm(one, two, dims):
    return lax.dot_general(one, two, dims, preferred_element_type=jnp.float32)


def lane_of(shape):
    return lax.broadcasted_iota(jnp.int32, shape, len(shape) - 1)


def swap_halves(part):
    return jnp.concatenate([part[:, HEAD_DIM:], part[:, :HEAD_DIM]], axis=1)


def pair_diagonal(part):
    lane = lane_of(part.shape)
    zero = jnp.zeros_like(part)
    return jnp.concatenate([jnp.where(lane < HEAD_DIM, part, zero), jnp.where(lane < HEAD_DIM, zero, part)], axis=0)


def own_half(ref, first, scale=1.0):
    full = ref[...].astype(jnp.float32) * scale
    part = jnp.where(first, full[:, :HALF], full[:, HALF:])
    last = jnp.concatenate([part[:, 256:], jnp.zeros_like(part[:, 256:])], axis=1)
    return [piece.astype(jnp.bfloat16) for piece in (part[:, :128], part[:, 128:256], last)]


def diagonal(one, two):
    right = jnp.zeros((one.shape[0], two.shape[1]), one.dtype)
    below = jnp.zeros((two.shape[0], one.shape[1]), one.dtype)
    return jnp.concatenate([jnp.concatenate([one, right], axis=1), jnp.concatenate([below, two], axis=1)], axis=0)


def masked(scores, limit_ref, block_rows):
    pieces = []
    for block in range(scores.shape[0] // block_rows):
        piece = scores[block * block_rows : (block + 1) * block_rows]
        row = lax.broadcasted_iota(jnp.int32, piece.shape, 0)
        pieces.append(jnp.where(row < limit_ref[block], piece, MASKED_SCORE))
    return jnp.concatenate(pieces, axis=0)


def turn_kernel(core_ref, x_ref, after_ref, out_ref, *, zs, ys):
    rows, unit = out_ref.shape[0], x_ref.shape[1] // (zs * ys)
    row = lax.broadcasted_iota(jnp.int32, (rows, 1), 0) + pl.program_id(0) * rows
    middle = row.astype(jnp.float32) + 0.5
    outer = (middle * (1.0 / (zs * unit))).astype(jnp.int32)
    piece = (middle * (1.0 / unit)).astype(jnp.int32)
    by_y = ((piece - outer * zs) * ys + outer) * unit + row - piece * unit
    source = jnp.where(core_ref[0] == 0, row, by_y)
    chosen = lane_of((rows, x_ref.shape[1])) == source
    out_ref[...] = mm(jnp.where(chosen, 1.0, 0.0).astype(jnp.bfloat16), x_ref[...], NT).astype(jnp.bfloat16)


def three_terms(value):
    terms = []
    for _ in range(3):
        term = value.astype(jnp.bfloat16).astype(jnp.float32)
        terms.append(term)
        value = value - term
    return terms


def lanes_left(value, by):
    return jnp.concatenate([value[..., by:], value[..., :by]], axis=-1)


def three_added(value):
    return value + lanes_left(value, 1) + lanes_left(value, 2)


def forward_kernel(
    core_ref, rep_ref, limit_ref, limit2_ref, xo_ref, xp_ref, *refs, block_rows, reps
):
    part_refs = refs[:reps]
    q_ref, kv_ref, stat_ref, w_ref, held_ref, sem = refs[reps:]
    share = part_refs[0].shape[0]
    rows = xo_ref.shape[0]
    fetch = pltpu.make_async_copy(xp_ref, held_ref, sem.at[0])
    fetch.start()
    for hop, part in enumerate(part_refs):
        start = pl.multiple_of(((rep_ref[0] + reps - hop) % reps) * share, share)
        w_ref[pl.ds(start, share), :] = part[...]
    q_parts = own_half(q_ref, core_ref[0] == 0, SCORE_SCALE)
    wide = diagonal(pair_diagonal(q_parts[0]), pair_diagonal(q_parts[1]))
    scores, last_scores = [], []
    for half, (x_ref, limits) in enumerate(((xo_ref, limit_ref), (held_ref, limit2_ref))):
        if half == 1:
            fetch.wait()
        kv = mm(x_ref[...], w_ref[...], NN).astype(jnp.bfloat16)
        kv_ref[half * rows : (half + 1) * rows, :] = kv
        scores.append(masked(mm(kv[:, :256], wide, NT), limits, block_rows))
        last_scores.append(masked(mm(kv[:, 256:384], q_parts[2], NT), limits, block_rows))
    outs, stats = [], []
    for parts, columns in ((scores, (384, 512)), (last_scores, (256,))):
        peak = jnp.maximum(*[jnp.max(part, axis=0, keepdims=True) for part in parts])
        total = jnp.zeros_like(peak)
        sums = [0.0] * len(columns)
        for half, part in enumerate(parts):
            p = jnp.exp(part - peak)
            total = total + jnp.sum(p, axis=0, keepdims=True)
            p = p.astype(jnp.bfloat16)
            span = p.shape[1] // len(columns)
            for index, column in enumerate(columns):
                values = kv_ref[half * rows : (half + 1) * rows, column : column + LANES]
                sums[index] = sums[index] + mm(p[:, index * span : (index + 1) * span], values, TN)
        outs += sums
        for head in range(peak.shape[1] // HEAD_DIM):
            cols = slice(head * HEAD_DIM, (head + 1) * HEAD_DIM)
            pad = jnp.zeros((2, HEAD_DIM), jnp.float32)
            stats.append(jnp.concatenate([*three_terms(total[:, cols]), *three_terms(peak[:, cols]), pad], axis=0))
    stats.append(jnp.zeros((LANES - 8 * OWN_HEADS, HEAD_DIM), jnp.float32))
    stats = jnp.concatenate(stats, axis=0).T
    lane = lane_of(stats.shape)
    for pair in range(2):
        both = outs[pair]
        stat_ref[:, pair, :] = jnp.where(lane < HEAD_DIM, both[:HEAD_DIM], both[HEAD_DIM:]).astype(jnp.bfloat16)
    stat_ref[:, 2, :] = jnp.where(lane < HEAD_DIM, stats, outs[2]).astype(jnp.bfloat16)
    stat_ref[:, 3, :] = jnp.zeros(stats.shape, jnp.bfloat16)


def of_heads(value, left, right):
    shape = value.shape
    return jnp.where(
        lane_of(shape) < HEAD_DIM,
        jnp.broadcast_to(value[..., 8 * left : 8 * left + 1], shape),
        jnp.broadcast_to(value[..., 8 * right : 8 * right + 1], shape),
    )


def combine_kernel(in_ref, out_ref, *, sources):
    terms = in_ref[...].astype(jnp.float32)
    rows = [terms[:, row, :] for row in range(3)]
    if sources != terms.shape[0]:
        rows = [row.reshape(sources, -1, LANES) for row in rows]
    added = three_added(rows[2])
    peak = lanes_left(added, 3)
    top = jnp.max(peak, axis=0, keepdims=True)
    weight = jnp.exp(peak - top)
    total = jnp.sum(added * weight, axis=0, keepdims=True)
    heads = ((0, 1), (2, 3), (4, 4))
    outs = []
    for row, pair in zip(rows, heads):
        outs.append(jnp.sum(row * of_heads(weight, *pair), axis=0, keepdims=True) / of_heads(total, *pair))
    lse = top + jnp.log(jnp.where(lane_of(total.shape) % 8 == 0, total, 1.0))
    first, second, third = three_terms(lse)
    kind = lane_of(lse.shape) % 8
    second = jnp.concatenate([second[..., -1:], second[..., :-1]], axis=-1)
    third = jnp.concatenate([third[..., -2:], third[..., :-2]], axis=-1)
    stat = jnp.where(kind == 0, first, jnp.where(kind == 1, second, jnp.where(kind == 2, third, 0.0)))
    outs[2] = jnp.where(lane_of(stat.shape) < HEAD_DIM, stat, outs[2])
    outs.append(jnp.zeros_like(stat))
    for row, out in enumerate(outs):
        out = jnp.broadcast_to(out, rows[0].shape).reshape(out_ref.shape[0], LANES)
        out_ref[:, row, :] = out.astype(jnp.bfloat16)


def backward_kernel(
    core_ref, limit_ref, limit2_ref, to_ref, tp_ref, kv_ref, q_ref, d_ref, merged_ref, attended_ref, grad_ref,
    rows_ref, turned_ref, sem, *, block_rows,
):
    half_rows = kv_ref.shape[0] // 2
    step = pl.program_id(0)

    @pl.when(step == 0)
    def _():
        fetches = [
            pltpu.make_async_copy(ref, turned_ref.at[half], sem.at[half]) for half, ref in enumerate((to_ref, tp_ref))
        ]
        for fetch in fetches:
            fetch.start()
        first = core_ref[0] == 0
        d_parts = own_half(d_ref, first)
        q_parts = own_half(q_ref, first, SCORE_SCALE)
        sides = [diagonal(pair_diagonal(q_parts[pair]), pair_diagonal(d_parts[pair])) for pair in range(2)]
        d_parts[2] = swap_halves(d_parts[2])
        sides.append(jnp.concatenate([q_parts[2], d_parts[2]], axis=0))
        merged = merged_ref[...].astype(jnp.float32)
        stat = three_added(merged[:, 2, :])
        lane = lane_of(stat.shape)
        for part in range(3):
            block = merged[:, part, :]
            product = d_parts[part].astype(jnp.float32) * block
            left = jnp.sum(jnp.where(lane < HEAD_DIM, product, 0.0), axis=1, keepdims=True)
            right = jnp.sum(jnp.where(lane < HEAD_DIM, 0.0, product), axis=1, keepdims=True)
            if part == 2:
                attended_ref[:, 256:] = swap_halves(block).astype(jnp.bfloat16)
                stat = jnp.where(lane == 33, right, stat)
            else:
                attended_ref[:, part * LANES : (part + 1) * LANES] = block.astype(jnp.bfloat16)
                stat = jnp.where(lane == 16 * part + 1, left, jnp.where(lane == 16 * part + 9, right, stat))
        stat = stat.T

        def row_of(heads, offset):
            return jnp.concatenate([stat[8 * head + offset : 8 * head + offset + 1] for head in heads], axis=1)

        for half, limits in enumerate((limit_ref, limit2_ref)):
            kv = kv_ref[half * half_rows : (half + 1) * half_rows, :]
            pairs = (
                (jnp.concatenate([kv[:, :128], kv[:, 384:512]], axis=1), (0, 1)),
                (jnp.concatenate([kv[:, 128:256], kv[:, 512:]], axis=1), (2, 3)),
                (kv[:, 256:384], (4,)),
            )
            target = slice(half * half_rows, (half + 1) * half_rows)
            for index, ((pair, heads), side) in enumerate(zip(pairs, sides)):
                span = HEAD_DIM * len(heads)
                both = mm(pair, side, NT)
                probs = jnp.exp(masked(both[:, :span], limits, block_rows) - row_of(heads, 0))
                score_grad = probs * (both[:, span:] - row_of(heads, 1))
                pair = jnp.concatenate([score_grad.astype(jnp.bfloat16), probs.astype(jnp.bfloat16)], axis=1)
                rows = mm(pair, side, NN).astype(jnp.bfloat16)
                if index == 2:
                    rows_ref[target, 256:384] = rows
                else:
                    rows_ref[target, index * LANES : (index + 1) * LANES] = rows[:, :LANES]
                    rows_ref[target, 384 + index * LANES : 512 + index * LANES] = rows[:, LANES:]
        for fetch in fetches:
            fetch.wait()

    size = grad_ref.shape[0]
    part = pl.ds(pl.multiple_of(step * size, size), size)
    grads = mm(turned_ref[0, part, :], rows_ref[:half_rows, :], NN) + mm(turned_ref[1, part, :], rows_ref[half_rows:, :], NN)
    grad_ref[...] = grads.astype(jnp.bfloat16)


def fold_kernel(in_ref, out_ref, *, length, reps):
    total = in_ref[0].astype(jnp.float32)
    for source in range(1, in_ref.shape[0]):
        total = total + in_ref[source].astype(jnp.float32)
    keys = total[:, :HALF]
    values = jnp.concatenate([total[:, 384:], total[:, HALF:384]], axis=1)
    pieces, padded, lanes = out_ref.shape
    width = 2 * HALF // reps
    for local in range(reps // 2):
        cols = slice(local * width, (local + 1) * width)
        part = jnp.concatenate([keys[:, cols], values[:, cols]], axis=1)
        if lanes != part.shape[1]:
            part = jnp.concatenate([part, jnp.zeros((part.shape[0], lanes - part.shape[1]), jnp.float32)], axis=1)
        for block in range(2 * pieces // reps):
            piece = part[block * length : (block + 1) * length]
            if padded != length:
                piece = jnp.concatenate([piece, jnp.zeros((padded - length, lanes), jnp.float32)], axis=0)
            out_ref[block * (reps // 2) + local] = piece.astype(jnp.bfloat16)


def whole(shape):
    return pl.BlockSpec(shape, lambda step, *_: (0,) * len(shape))


def row_block(rows, cols):
    return pl.BlockSpec((rows, cols), lambda step, *_: (step, 0))


def shaped(shape, dtype=jnp.bfloat16):
    return jax.ShapeDtypeStruct(shape, dtype)


def call(kernel, name, scalars, grid, in_specs, out_specs, out_shape, flops, nbytes, scratch=(), vmem=VMEM_LIMIT):
    return pl.pallas_call(
        kernel,
        name=name,
        out_shape=out_shape,
        grid_spec=pltpu.PrefetchScalarGridSpec(
            num_scalar_prefetch=scalars, grid=grid, in_specs=in_specs, out_specs=out_specs, scratch_shapes=scratch
        ),
        compiler_params=pltpu.CompilerParams(dimension_semantics=("arbitrary",), vmem_limit_bytes=vmem),
        cost_estimate=pl.CostEstimate(flops=flops, bytes_accessed=nbytes, transcendentals=0),
    )


def device(z, y, c, x):
    _, ys, cs, xs = GRID
    return ((z * ys + y) * cs + c) * xs + x


def first_groups():
    zs, ys, _, xs = GRID
    groups = []
    for x in range(xs):
        groups += [[device(z, y, 0, x) for z in range(zs)] for y in range(ys)]
        groups += [[device(z, y, 1, x) for y in range(ys)] for z in range(zs)]
    return groups


def second_groups():
    zs, ys, _, xs = GRID
    groups = [[device(z, y, 0, x) for y in range(ys) for x in range(xs)] for z in range(zs)]
    groups += [[device(z, y, 1, x) for z in range(zs) for x in range(xs)] for y in range(ys)]
    return groups


def padded_to(count, unit):
    return -(-count // unit) * unit


def body(tile_embed, block_slide, block_rank, tile_count, queries, w_key, w_value, d_attended):
    zs, ys, _, xs = GRID
    _, slots, block_rows, width_in = tile_embed.shape
    rows = slots * block_rows
    latents, width = queries.shape
    core = lax.axis_index("c")
    first = core == 0
    both_rows = 2 * rows
    big_flops = 2 * both_rows * width_in * width
    core_arg = core.astype(jnp.int32)[None]
    rep_arg = lax.axis_index("x").astype(jnp.int32)[None]
    anywhere = pl.BlockSpec(memory_space=pl.ANY)
    in_vmem = pl.BlockSpec(memory_space=pltpu.VMEM)
    in_hbm = pl.BlockSpec(memory_space=pltpu.HBM)

    def partner(value):
        return lax.ppermute(value, "c", [(0, 1), (1, 0)])

    key_half = jnp.where(first, w_key[:, :HALF], w_key[:, HALF:])
    value_half = jnp.where(first, w_value[:, :HALF], w_value[:, HALF:])
    w_own = jnp.concatenate([key_half, value_half[:, 256:], value_half[:, :256]], axis=1)
    w_parts = [w_own]
    for hop in range(1, xs):
        w_parts.append(lax.ppermute(w_own, "x", [(x, (x + hop) % xs) for x in range(xs)]))

    x_own = tile_embed.reshape(rows, width_in)
    x_part = partner(x_own)
    limits = jnp.where(block_slide[0] >= 0, tile_count[0, 0] - block_rank[0] * block_rows, 0)
    limits2 = partner(limits)

    stat_shape = (latents, 4, LANES)
    kv, stats = call(
        lambda *refs: forward_kernel(*refs, block_rows=block_rows, reps=xs), "forward_pass", 4, (1,),
        [in_vmem, in_hbm, *[in_vmem] * xs, whole(queries.shape)], (in_vmem, whole(stat_shape)),
        (shaped((both_rows, width)), shaped(stat_shape)), big_flops, 10 << 20,
        [
            pltpu.VMEM((width_in, width), jnp.bfloat16), pltpu.VMEM((rows, width_in), jnp.bfloat16),
            pltpu.SemaphoreType.DMA((1,)),
        ],
    )(core_arg, rep_arg, limits, limits2, x_own, x_part, *w_parts, queries)

    def turned(tiles, name):
        return call(
            lambda *refs: turn_kernel(*refs, zs=zs, ys=ys), name, 1, (5,), [in_vmem, anywhere],
            row_block(width_in // 5, rows), shaped((width_in, rows)), 2 * rows * width_in * width_in, 5 << 20,
        )(core_arg, tiles, stats)

    turned_own = turned(x_own, "turn_own")
    turned_part = turned(x_part, "turn_partner")

    chips = ("z", "y")
    stats = lax.all_to_all(stats, chips, 0, 0, tiled=True)
    merged = call(
        lambda *refs: combine_kernel(*refs, sources=zs * ys), "combine", 0, (1,),
        [whole(stat_shape)], whole(stat_shape), shaped(stat_shape), stats.size * 4, stats.size * 4,
    )(stats)
    merged = lax.all_to_all(merged, chips, 0, 0, tiled=True)

    d_out = d_attended.reshape(latents, width)
    attended, grads = call(
        lambda *refs: backward_kernel(*refs, block_rows=block_rows), "backward_pass", 3, (2,),
        [in_hbm, in_hbm, in_vmem, whole(queries.shape), whole(d_out.shape), whole(stat_shape)],
        (whole((latents, 3 * LANES)), row_block(width_in // 2, width)),
        (shaped((latents, 3 * LANES)), shaped((width_in, width))),
        big_flops, 10 << 20,
        [
            pltpu.VMEM((both_rows, width), jnp.bfloat16), pltpu.VMEM((2, width_in, rows), jnp.bfloat16),
            pltpu.SemaphoreType.DMA((2,)),
        ],
        58 << 20,
    )(core_arg, limits, limits2, turned_own, turned_part, kv, queries, d_out, merged)
    mine = attended[:, :HALF]
    theirs = partner(mine)
    attended = jnp.where(first, jnp.concatenate([mine, theirs], axis=1), jnp.concatenate([theirs, mine], axis=1))

    received = lax.all_to_all(grads, AXES, 0, 0, axis_index_groups=first_groups(), tiled=True)
    received = received.reshape(zs, width_in // zs, width)
    length = width_in // (2 * zs * ys)
    share = width // xs
    chunk = (ys * xs, padded_to(length, 16), padded_to(2 * share, LANES))
    pieces = call(
        lambda *refs: fold_kernel(*refs, length=length, reps=xs), "fold", 0, (1,), [whole(received.shape)],
        whole(chunk), shaped(chunk), received.size, received.size * 2,
    )(received)
    received = lax.all_to_all(pieces, AXES, 0, 0, axis_index_groups=second_groups(), tiled=True)
    total = jnp.sum(received.astype(jnp.float32), axis=0)[:length, : 2 * share]
    half = xs // 2
    home = [(c * xs + x, (x // half) * xs + c * half + x % half) for c in range(2) for x in range(xs)]
    total = lax.ppermute(total, ("c", "x"), home)
    return (attended.reshape(1, 1, latents, width), total[:, :share], total[:, share:])


def solution(mesh):
    grid = Mesh(mesh.devices.reshape(GRID), AXES)
    placed = (
        P("x", TILES, None, None),
        P("x", TILES),
        P("x", TILES),
        P("x", None),
        P(),
        P("x", None),
        P("x", None),
        P("x", None, None, None),
    )
    return jax.shard_map(
        body,
        mesh=grid,
        in_specs=placed,
        out_specs=(P("x", None, None, None), P(TILES, "x"), P(TILES, "x")),
        check_vma=False,
    )
```

```python
import jax
import jax.numpy as jnp
from jax import lax
from jax.experimental import pallas as pl
from jax.experimental.pallas import tpu as pltpu
from jax.sharding import Mesh, PartitionSpec as P

HEAD_DIM = 64
OWN_HEADS = 5
HALF = OWN_HEADS * HEAD_DIM
LANES = 128
SCORE_SCALE = 0.125
MASKED_SCORE = -1e30

VMEM_LIMIT = 59 << 20
FORWARD_LIMIT = 32 << 20

GRID = (8, 8, 2, 4)
AXES = ("z", "y", "c", "x")
TILES = ("z", "y", "c")

NT = (((1,), (1,)), ((), ()))
TN = (((0,), (0,)), ((), ()))
NN = (((1,), (0,)), ((), ()))


def mm(one, two, dims):
    return lax.dot_general(one, two, dims, preferred_element_type=jnp.float32)


def lane_of(shape):
    return lax.broadcasted_iota(jnp.int32, shape, len(shape) - 1)


def swap_halves(part):
    return jnp.concatenate([part[:, HEAD_DIM:], part[:, :HEAD_DIM]], axis=1)


def pair_diagonal(part):
    lane = lane_of(part.shape)
    zero = jnp.zeros_like(part)
    return jnp.concatenate([jnp.where(lane < HEAD_DIM, part, zero), jnp.where(lane < HEAD_DIM, zero, part)], axis=0)


def own_half(ref, first):
    full = ref[...].astype(jnp.float32)
    part = jnp.where(first, full[:, :HALF], full[:, HALF:])
    last = jnp.concatenate([part[:, 256:], jnp.zeros_like(part[:, 256:])], axis=1)
    return [piece.astype(jnp.bfloat16) for piece in (part[:, :128], part[:, 128:256], last)]


def diagonal(one, two):
    right = jnp.zeros((one.shape[0], two.shape[1]), one.dtype)
    below = jnp.zeros((two.shape[0], one.shape[1]), one.dtype)
    return jnp.concatenate([jnp.concatenate([one, right], axis=1), jnp.concatenate([below, two], axis=1)], axis=0)


def masked(scores, limit_ref, block_rows):
    pieces = []
    for block in range(scores.shape[0] // block_rows):
        piece = scores[block * block_rows : (block + 1) * block_rows]
        row = lax.broadcasted_iota(jnp.int32, piece.shape, 0)
        pieces.append(jnp.where(row < limit_ref[block], piece, MASKED_SCORE))
    return jnp.concatenate(pieces, axis=0)


def turn_kernel(core_ref, x_ref, after_ref, out_ref, token_ref, *, zs, ys):
    rows, unit = out_ref.shape[0], x_ref.shape[1] // (zs * ys)
    row = lax.broadcasted_iota(jnp.int32, (rows, 1), 0) + pl.program_id(0) * rows
    middle = row.astype(jnp.float32) + 0.5
    outer = (middle * (1.0 / (zs * unit))).astype(jnp.int32)
    piece = (middle * (1.0 / unit)).astype(jnp.int32)
    by_y = ((piece - outer * zs) * ys + outer) * unit + row - piece * unit
    source = jnp.where(core_ref[0] == 0, row, by_y)
    chosen = lane_of((rows, x_ref.shape[1])) == source
    out_ref[...] = mm(jnp.where(chosen, 1.0, 0.0).astype(jnp.bfloat16), x_ref[...], NT).astype(jnp.bfloat16)
    token_ref[...] = jnp.zeros_like(token_ref)


def three_terms(value):
    terms = []
    for _ in range(3):
        term = value.astype(jnp.bfloat16).astype(jnp.float32)
        terms.append(term)
        value = value - term
    return terms


def lanes_left(value, by):
    return jnp.concatenate([value[..., by:], value[..., :by]], axis=-1)


def three_added(value):
    return value + lanes_left(value, 1) + lanes_left(value, 2)


def forward_kernel(
    core_ref, rep_ref, limit_ref, limit2_ref, xo_ref, xp_ref, *refs, block_rows, reps
):
    part_refs = refs[: 2 * reps]
    q_ref, out_ref, stat_ref, w_ref, held_ref, kv_ref, sem, out_sem = refs[2 * reps :]
    share = part_refs[0].shape[0]
    rows = xo_ref.shape[0]
    stores = []
    fetch = pltpu.make_async_copy(xp_ref, held_ref, sem.at[0])
    fetch.start()
    for index, part in enumerate(part_refs):
        origin = (rep_ref[0] + reps - index // 2) % reps
        w_ref[pl.ds(pl.multiple_of((2 * origin + index % 2) * share, share), share), :] = part[...]
    q_parts = own_half(q_ref, core_ref[0] == 0)
    wide = diagonal(pair_diagonal(q_parts[0]), pair_diagonal(q_parts[1]))
    scores, last_scores = [], []
    for half, (x_ref, limits) in enumerate(((xo_ref, limit_ref), (held_ref, limit2_ref))):
        if half == 1:
            fetch.wait()
        kv = mm(x_ref[...], w_ref[...], NN).astype(jnp.bfloat16)
        kv_ref[half * rows : (half + 1) * rows, :] = kv
        place = pl.ds(half * rows, rows)
        stores.append(pltpu.make_async_copy(kv_ref.at[place, :], out_ref.at[place, :], out_sem.at[half]))
        stores[half].start()
        scores.append(masked(mm(kv[:, :256], wide, NT), limits, block_rows))
        last_scores.append(masked(mm(kv[:, 256:384], q_parts[2], NT), limits, block_rows))
    outs, stats = [], []
    for parts, columns in ((scores, (384, 512)), (last_scores, (256,))):
        peak = jnp.maximum(*[jnp.max(part, axis=0, keepdims=True) for part in parts])
        total = jnp.zeros_like(peak)
        sums = [0.0] * len(columns)
        for half, part in enumerate(parts):
            p = jnp.exp(part - peak)
            total = total + jnp.sum(p, axis=0, keepdims=True)
            p = p.astype(jnp.bfloat16)
            span = p.shape[1] // len(columns)
            for index, column in enumerate(columns):
                values = kv_ref[half * rows : (half + 1) * rows, column : column + LANES]
                sums[index] = sums[index] + mm(p[:, index * span : (index + 1) * span], values, TN)
        outs += sums
        for head in range(peak.shape[1] // HEAD_DIM):
            cols = slice(head * HEAD_DIM, (head + 1) * HEAD_DIM)
            pad = jnp.zeros((2, HEAD_DIM), jnp.float32)
            stats.append(jnp.concatenate([*three_terms(total[:, cols]), *three_terms(peak[:, cols]), pad], axis=0))
    stats.append(jnp.zeros((LANES - 8 * OWN_HEADS, HEAD_DIM), jnp.float32))
    stats = jnp.concatenate(stats, axis=0).T
    lane = lane_of(stats.shape)
    for pair in range(2):
        both = outs[pair]
        stat_ref[:, pair, :] = jnp.where(lane < HEAD_DIM, both[:HEAD_DIM], both[HEAD_DIM:]).astype(jnp.bfloat16)
    stat_ref[:, 2, :] = jnp.where(lane < HEAD_DIM, stats, outs[2]).astype(jnp.bfloat16)
    stat_ref[:, 3, :] = jnp.zeros(stats.shape, jnp.bfloat16)
    for store in stores:
        store.wait()


def of_heads(value, left, right):
    shape = value.shape
    return jnp.where(
        lane_of(shape) < HEAD_DIM,
        jnp.broadcast_to(value[..., 8 * left : 8 * left + 1], shape),
        jnp.broadcast_to(value[..., 8 * right : 8 * right + 1], shape),
    )


def combine_kernel(in_ref, own_ref, partner_ref, out_ref, *, sources):
    terms = in_ref[...].astype(jnp.float32)
    rows = [terms[:, row, :] for row in range(3)]
    if sources != terms.shape[0]:
        rows = [row.reshape(sources, -1, LANES) for row in rows]
    added = three_added(rows[2])
    peak = lanes_left(added, 3)
    top = jnp.max(peak, axis=0, keepdims=True)
    weight = jnp.exp(peak - top)
    total = jnp.sum(added * weight, axis=0, keepdims=True)
    heads = ((0, 1), (2, 3), (4, 4))
    outs = []
    for row, pair in zip(rows, heads):
        outs.append(jnp.sum(row * of_heads(weight, *pair), axis=0, keepdims=True) / of_heads(total, *pair))
    lse = top + jnp.log(jnp.where(lane_of(total.shape) % 8 == 0, total, 1.0))
    first, second, third = three_terms(lse)
    kind = lane_of(lse.shape) % 8
    second = jnp.concatenate([second[..., -1:], second[..., :-1]], axis=-1)
    third = jnp.concatenate([third[..., -2:], third[..., :-2]], axis=-1)
    stat = jnp.where(kind == 0, first, jnp.where(kind == 1, second, jnp.where(kind == 2, third, 0.0)))
    outs[2] = jnp.where(lane_of(stat.shape) < HEAD_DIM, stat, outs[2])
    outs.append(jnp.zeros_like(stat))
    for row, out in enumerate(outs):
        out = jnp.broadcast_to(out, rows[0].shape).reshape(out_ref.shape[0], LANES)
        out_ref[:, row, :] = out.astype(jnp.bfloat16)


def backward_kernel(
    core_ref, limit_ref, limit2_ref, to_ref, tp_ref, in_ref, q_ref, d_ref, merged_ref, attended_ref, grad_ref,
    rows_ref, turned_ref, kv_ref, sem, kv_sem, *, block_rows,
):
    half_rows = kv_ref.shape[0] // 2
    step = pl.program_id(0)

    @pl.when(step == 0)
    def _():
        fetches = [
            pltpu.make_async_copy(ref, turned_ref.at[half], sem.at[half]) for half, ref in enumerate((to_ref, tp_ref))
        ]
        places = [pl.ds(half * half_rows, half_rows) for half in range(2)]
        loads = [
            pltpu.make_async_copy(in_ref.at[place, :], kv_ref.at[place, :], kv_sem.at[half])
            for half, place in enumerate(places)
        ]
        for fetch in (*loads, *fetches):
            fetch.start()
        first = core_ref[0] == 0
        d_parts = own_half(d_ref, first)
        q_parts = own_half(q_ref, first)
        sides = [diagonal(pair_diagonal(q_parts[pair]), pair_diagonal(d_parts[pair])) for pair in range(2)]
        d_parts[2] = swap_halves(d_parts[2])
        sides.append(jnp.concatenate([q_parts[2], d_parts[2]], axis=0))
        merged = merged_ref[...].astype(jnp.float32)
        stat = three_added(merged[:, 2, :])
        lane = lane_of(stat.shape)
        for part in range(3):
            block = merged[:, part, :]
            product = d_parts[part].astype(jnp.float32) * block
            left = jnp.sum(jnp.where(lane < HEAD_DIM, product, 0.0), axis=1, keepdims=True)
            right = jnp.sum(jnp.where(lane < HEAD_DIM, 0.0, product), axis=1, keepdims=True)
            if part == 2:
                attended_ref[:, 256:] = swap_halves(block).astype(jnp.bfloat16)
                stat = jnp.where(lane == 33, right, stat)
            else:
                attended_ref[:, part * LANES : (part + 1) * LANES] = block.astype(jnp.bfloat16)
                stat = jnp.where(lane == 16 * part + 1, left, jnp.where(lane == 16 * part + 9, right, stat))
        stat = stat.T

        def row_of(heads, offset):
            return jnp.concatenate([stat[8 * head + offset : 8 * head + offset + 1] for head in heads], axis=1)

        for half, limits in enumerate((limit_ref, limit2_ref)):
            loads[half].wait()
            kv = kv_ref[half * half_rows : (half + 1) * half_rows, :]
            pairs = (
                (jnp.concatenate([kv[:, :128], kv[:, 384:512]], axis=1), (0, 1)),
                (jnp.concatenate([kv[:, 128:256], kv[:, 512:]], axis=1), (2, 3)),
                (kv[:, 256:384], (4,)),
            )
            target = slice(half * half_rows, (half + 1) * half_rows)
            for index, ((pair, heads), side) in enumerate(zip(pairs, sides)):
                span = HEAD_DIM * len(heads)
                both = mm(pair, side, NT)
                probs = jnp.exp(masked(both[:, :span], limits, block_rows) - row_of(heads, 0))
                score_grad = probs * (both[:, span:] - row_of(heads, 1))
                pair = jnp.concatenate([score_grad.astype(jnp.bfloat16), probs.astype(jnp.bfloat16)], axis=1)
                rows = mm(pair, side, NN).astype(jnp.bfloat16)
                if index == 2:
                    rows_ref[target, 256:384] = rows
                else:
                    rows_ref[target, index * LANES : (index + 1) * LANES] = rows[:, :LANES]
                    rows_ref[target, 384 + index * LANES : 512 + index * LANES] = rows[:, LANES:]
        for fetch in fetches:
            fetch.wait()

    size = grad_ref.shape[0]
    part = pl.ds(pl.multiple_of(step * size, size), size)
    grads = mm(turned_ref[0, part, :], rows_ref[:half_rows, :], NN) + mm(turned_ref[1, part, :], rows_ref[half_rows:, :], NN)
    grad_ref[...] = grads.astype(jnp.bfloat16)


def fold_kernel(in_ref, out_ref, *, length, reps):
    total = in_ref[0].astype(jnp.float32)
    for source in range(1, in_ref.shape[0]):
        total = total + in_ref[source].astype(jnp.float32)
    keys = total[:, :HALF]
    values = jnp.concatenate([total[:, 384:], total[:, HALF:384]], axis=1)
    pieces, padded, lanes = out_ref.shape
    width = 2 * HALF // reps
    for local in range(reps // 2):
        cols = slice(local * width, (local + 1) * width)
        part = jnp.concatenate([keys[:, cols], values[:, cols]], axis=1)
        if lanes != part.shape[1]:
            part = jnp.concatenate([part, jnp.zeros((part.shape[0], lanes - part.shape[1]), jnp.float32)], axis=1)
        for block in range(2 * pieces // reps):
            piece = part[block * length : (block + 1) * length]
            if padded != length:
                piece = jnp.concatenate([piece, jnp.zeros((padded - length, lanes), jnp.float32)], axis=0)
            out_ref[block * (reps // 2) + local] = piece.astype(jnp.bfloat16)


def whole(shape):
    return pl.BlockSpec(shape, lambda step, *_: (0,) * len(shape))


def row_block(rows, cols):
    return pl.BlockSpec((rows, cols), lambda step, *_: (step, 0))


def shaped(shape, dtype=jnp.bfloat16):
    return jax.ShapeDtypeStruct(shape, dtype)


def call(kernel, name, scalars, grid, in_specs, out_specs, out_shape, flops, nbytes, scratch=(), vmem=VMEM_LIMIT):
    return pl.pallas_call(
        kernel,
        name=name,
        out_shape=out_shape,
        grid_spec=pltpu.PrefetchScalarGridSpec(
            num_scalar_prefetch=scalars, grid=grid, in_specs=in_specs, out_specs=out_specs, scratch_shapes=scratch
        ),
        compiler_params=pltpu.CompilerParams(dimension_semantics=("arbitrary",), vmem_limit_bytes=vmem),
        cost_estimate=pl.CostEstimate(flops=flops, bytes_accessed=nbytes, transcendentals=0),
    )


def device(z, y, c, x):
    _, ys, cs, xs = GRID
    return ((z * ys + y) * cs + c) * xs + x


def first_groups():
    zs, ys, _, xs = GRID
    groups = []
    for x in range(xs):
        groups += [[device(z, y, 0, x) for z in range(zs)] for y in range(ys)]
        groups += [[device(z, y, 1, x) for y in range(ys)] for z in range(zs)]
    return groups


def second_groups():
    zs, ys, _, xs = GRID
    groups = [[device(z, y, 0, x) for y in range(ys) for x in range(xs)] for z in range(zs)]
    groups += [[device(z, y, 1, x) for z in range(zs) for x in range(xs)] for y in range(ys)]
    return groups


def padded_to(count, unit):
    return -(-count // unit) * unit


def body(tile_embed, block_slide, block_rank, tile_count, queries, w_key, w_value, d_attended):
    zs, ys, _, xs = GRID
    _, slots, block_rows, width_in = tile_embed.shape
    rows = slots * block_rows
    latents, width = queries.shape
    core = lax.axis_index("c")
    first = core == 0
    both_rows = 2 * rows
    big_flops = 2 * both_rows * width_in * width
    core_arg = core.astype(jnp.int32)[None]
    rep_arg = lax.axis_index("x").astype(jnp.int32)[None]
    anywhere = pl.BlockSpec(memory_space=pl.ANY)
    in_vmem = pl.BlockSpec(memory_space=pltpu.VMEM)
    in_hbm = pl.BlockSpec(memory_space=pltpu.HBM)

    def partner(value):
        return lax.ppermute(value, "c", [(0, 1), (1, 0)])

    def own_columns(rows):
        key_half = jnp.where(first, w_key[rows, :HALF], w_key[rows, HALF:])
        value_half = jnp.where(first, w_value[rows, :HALF], w_value[rows, HALF:])
        return jnp.concatenate([key_half, value_half[:, 256:], value_half[:, :256]], axis=1)

    def shifted(value, by):
        return lax.ppermute(value, "x", [(x, (x + by) % xs) for x in range(xs)])

    share = w_key.shape[0] // 2
    top, bottom = own_columns(slice(0, share)), own_columns(slice(share, None))
    left_top, right_bottom = shifted(top, 1), shifted(bottom, -1)
    if xs == 4:
        left_bottom, right_top = shifted(bottom, 1), shifted(top, -1)
        w_parts = [
            top, bottom, left_top, left_bottom, shifted(left_top, 1), shifted(right_bottom, -1), right_top, right_bottom
        ]
    else:
        w_parts = [top, bottom, left_top, right_bottom]
    q_scaled = (queries.astype(jnp.float32) * SCORE_SCALE).astype(jnp.bfloat16)

    x_own = tile_embed.reshape(rows, width_in)
    x_part = partner(x_own)
    limits = jnp.where(block_slide[0] >= 0, tile_count[0, 0] - block_rank[0] * block_rows, 0)
    limits2 = partner(limits)

    stat_shape = (latents, 4, LANES)
    kv, stats = call(
        lambda *refs: forward_kernel(*refs, block_rows=block_rows, reps=xs), "forward_pass", 4, (1,),
        [in_vmem, in_hbm, *[in_vmem] * (2 * xs), in_vmem], (in_hbm, in_vmem),
        (pltpu.HBM((both_rows, width), jnp.bfloat16), shaped(stat_shape)), big_flops, 10 << 20,
        [
            pltpu.VMEM((width_in, width), jnp.bfloat16), pltpu.VMEM((rows, width_in), jnp.bfloat16),
            pltpu.VMEM((both_rows, width), jnp.bfloat16), pltpu.SemaphoreType.DMA((1,)), pltpu.SemaphoreType.DMA((2,)),
        ],
        FORWARD_LIMIT,
    )(core_arg, rep_arg, limits, limits2, x_own, x_part, *w_parts, q_scaled)

    def turned(tiles, name):
        return call(
            lambda *refs: turn_kernel(*refs, zs=zs, ys=ys), name, 1, (5,), [in_vmem, anywhere],
            (row_block(width_in // 5, rows), whole((8, LANES))), (shaped((width_in, rows)), shaped((8, LANES), jnp.float32)),
            2 * rows * width_in * width_in, 5 << 20,
        )(core_arg, tiles, stats)

    turned_own, own_done = turned(x_own, "turn_own")
    turned_part, part_done = turned(x_part, "turn_partner")

    chips = ("z", "y")
    stats = lax.all_to_all(stats, chips, 0, 0, tiled=True)
    merged = call(
        lambda *refs: combine_kernel(*refs, sources=zs * ys), "combine", 0, (1,),
        [in_vmem] * 3, in_vmem, shaped(stat_shape), stats.size * 4, stats.size * 4, (), FORWARD_LIMIT,
    )(stats, own_done, part_done)
    merged = lax.all_to_all(merged, chips, 0, 0, tiled=True)

    d_out = d_attended.reshape(latents, width)
    attended, grads = call(
        lambda *refs: backward_kernel(*refs, block_rows=block_rows), "backward_pass", 3, (2,),
        [in_hbm, in_hbm, in_hbm, in_vmem, whole(d_out.shape), in_vmem],
        (whole((latents, 3 * LANES)), row_block(width_in // 2, width)),
        (shaped((latents, 3 * LANES)), shaped((width_in, width))),
        big_flops, 10 << 20,
        [
            pltpu.VMEM((both_rows, width), jnp.bfloat16), pltpu.VMEM((2, width_in, rows), jnp.bfloat16),
            pltpu.VMEM((both_rows, width), jnp.bfloat16), pltpu.SemaphoreType.DMA((2,)), pltpu.SemaphoreType.DMA((2,)),
        ],
        VMEM_LIMIT,
    )(core_arg, limits, limits2, turned_own, turned_part, kv, q_scaled, d_out, merged)
    mine = attended[:, :HALF]
    theirs = partner(mine)
    attended = jnp.where(first, jnp.concatenate([mine, theirs], axis=1), jnp.concatenate([theirs, mine], axis=1))

    received = lax.all_to_all(grads, AXES, 0, 0, axis_index_groups=first_groups(), tiled=True)
    received = received.reshape(zs, width_in // zs, width)
    length = width_in // (2 * zs * ys)
    share = width // xs
    chunk = (ys * xs, padded_to(length, 16), padded_to(2 * share, LANES))
    pieces = call(
        lambda *refs: fold_kernel(*refs, length=length, reps=xs), "fold", 0, (1,), [whole(received.shape)],
        whole(chunk), shaped(chunk), received.size, received.size * 2,
    )(received)
    received = lax.all_to_all(pieces, AXES, 0, 0, axis_index_groups=second_groups(), tiled=True)
    total = jnp.sum(received.astype(jnp.float32), axis=0)[:length, : 2 * share]
    half = xs // 2
    home = [(c * xs + x, (x // half) * xs + c * half + x % half) for c in range(2) for x in range(xs)]
    total = lax.ppermute(total, ("c", "x"), home)
    return (attended.reshape(1, 1, latents, width), total[:, :share], total[:, share:])


def solution(mesh):
    grid = Mesh(mesh.devices.reshape(GRID), AXES)
    placed = (
        P("x", TILES, None, None),
        P("x", TILES),
        P("x", TILES),
        P("x", None),
        P(),
        P("x", None),
        P("x", None),
        P("x", None, None, None),
    )
    return jax.shard_map(
        body,
        mesh=grid,
        in_specs=placed,
        out_specs=(P("x", None, None, None), P(TILES, "x"), P(TILES, "x")),
        check_vma=False,
    )
```

```python
import jax
import jax.numpy as jnp
from jax import lax
from jax.experimental import pallas as pl
from jax.experimental.pallas import tpu as pltpu
from jax.sharding import Mesh, PartitionSpec as P

HEAD_DIM = 64
OWN_HEADS = 5
HALF = OWN_HEADS * HEAD_DIM
LANES = 128
SCORE_SCALE = 0.125
MASKED_SCORE = -1e30

VMEM_LIMIT = 59 << 20
FORWARD_LIMIT = 32 << 20
BACKWARD_LIMIT = 48 << 20

GRID = (8, 8, 2, 4)
AXES = ("z", "y", "c", "x")
TILES = ("z", "y", "c")

NT = (((1,), (1,)), ((), ()))
TN = (((0,), (0,)), ((), ()))
NN = (((1,), (0,)), ((), ()))


def mm(one, two, dims):
    return lax.dot_general(one, two, dims, preferred_element_type=jnp.float32)


def lane_of(shape):
    return lax.broadcasted_iota(jnp.int32, shape, len(shape) - 1)


def swap_halves(part):
    return jnp.concatenate([part[:, HEAD_DIM:], part[:, :HEAD_DIM]], axis=1)


def pair_diagonal(part):
    lane = lane_of(part.shape)
    zero = jnp.zeros_like(part)
    return jnp.concatenate([jnp.where(lane < HEAD_DIM, part, zero), jnp.where(lane < HEAD_DIM, zero, part)], axis=0)


def own_half(ref, first):
    full = ref[...].astype(jnp.float32)
    part = jnp.where(first, full[:, :HALF], full[:, HALF:])
    last = jnp.concatenate([part[:, 256:], jnp.zeros_like(part[:, 256:])], axis=1)
    return [piece.astype(jnp.bfloat16) for piece in (part[:, :128], part[:, 128:256], last)]


def diagonal(one, two):
    right = jnp.zeros((one.shape[0], two.shape[1]), one.dtype)
    below = jnp.zeros((two.shape[0], one.shape[1]), one.dtype)
    return jnp.concatenate([jnp.concatenate([one, right], axis=1), jnp.concatenate([below, two], axis=1)], axis=0)


def masked(scores, limit_ref, block_rows):
    pieces = []
    for block in range(scores.shape[0] // block_rows):
        piece = scores[block * block_rows : (block + 1) * block_rows]
        row = lax.broadcasted_iota(jnp.int32, piece.shape, 0)
        pieces.append(jnp.where(row < limit_ref[block], piece, MASKED_SCORE))
    return jnp.concatenate(pieces, axis=0)


def turn_kernel(core_ref, x_ref, after_ref, out_ref, token_ref, *, zs, ys):
    rows, unit = out_ref.shape[0], x_ref.shape[1] // (zs * ys)
    row = lax.broadcasted_iota(jnp.int32, (rows, 1), 0) + pl.program_id(0) * rows
    middle = row.astype(jnp.float32) + 0.5
    outer = (middle * (1.0 / (zs * unit))).astype(jnp.int32)
    piece = (middle * (1.0 / unit)).astype(jnp.int32)
    by_y = ((piece - outer * zs) * ys + outer) * unit + row - piece * unit
    source = jnp.where(core_ref[0] == 0, row, by_y)
    chosen = lane_of((rows, x_ref.shape[1])) == source
    out_ref[...] = mm(jnp.where(chosen, 1.0, 0.0).astype(jnp.bfloat16), x_ref[...], NT).astype(jnp.bfloat16)
    token_ref[...] = jnp.zeros_like(token_ref)


def three_terms(value):
    terms = []
    for _ in range(3):
        term = value.astype(jnp.bfloat16).astype(jnp.float32)
        terms.append(term)
        value = value - term
    return terms


def lanes_left(value, by):
    return jnp.concatenate([value[..., by:], value[..., :by]], axis=-1)


def three_added(value):
    return value + lanes_left(value, 1) + lanes_left(value, 2)


def forward_kernel(
    core_ref, rep_ref, limit_ref, limit2_ref, xo_ref, xp_ref, *refs, block_rows, reps
):
    part_refs = refs[:reps]
    q_ref, _, out_ref, stat_ref, w_ref, held_ref, kv_ref, sem, out_sem = refs[reps:]
    share = part_refs[0].shape[0]
    rows = xo_ref.shape[0]
    stores = []
    fetch = pltpu.make_async_copy(xp_ref, held_ref, sem.at[0])
    fetch.start()
    for index, part in enumerate(part_refs):
        origin = (rep_ref[0] + index) % reps
        w_ref[pl.ds(pl.multiple_of(origin * share, share), share), :] = part[...]
    q_parts = own_half(q_ref, core_ref[0] == 0)
    wide = diagonal(pair_diagonal(q_parts[0]), pair_diagonal(q_parts[1]))
    scores, last_scores = [], []
    for half, (x_ref, limits) in enumerate(((xo_ref, limit_ref), (held_ref, limit2_ref))):
        if half == 1:
            fetch.wait()
        kv = mm(x_ref[...], w_ref[...], NN).astype(jnp.bfloat16)
        kv_ref[half * rows : (half + 1) * rows, :] = kv
        place = pl.ds(half * rows, rows)
        stores.append(pltpu.make_async_copy(kv_ref.at[place, :], out_ref.at[place, :], out_sem.at[half]))
        stores[half].start()
        scores.append(masked(mm(kv[:, :256], wide, NT), limits, block_rows))
        last_scores.append(masked(mm(kv[:, 256:384], q_parts[2], NT), limits, block_rows))
    outs, stats = [], []
    for parts, columns in ((scores, (384, 512)), (last_scores, (256,))):
        peak = jnp.maximum(*[jnp.max(part, axis=0, keepdims=True) for part in parts])
        total = jnp.zeros_like(peak)
        sums = [0.0] * len(columns)
        for half, part in enumerate(parts):
            p = jnp.exp(part - peak)
            total = total + jnp.sum(p, axis=0, keepdims=True)
            p = p.astype(jnp.bfloat16)
            span = p.shape[1] // len(columns)
            for index, column in enumerate(columns):
                values = kv_ref[half * rows : (half + 1) * rows, column : column + LANES]
                sums[index] = sums[index] + mm(p[:, index * span : (index + 1) * span], values, TN)
        outs += sums
        for head in range(peak.shape[1] // HEAD_DIM):
            cols = slice(head * HEAD_DIM, (head + 1) * HEAD_DIM)
            pad = jnp.zeros((2, HEAD_DIM), jnp.float32)
            stats.append(jnp.concatenate([*three_terms(total[:, cols]), *three_terms(peak[:, cols]), pad], axis=0))
    stats.append(jnp.zeros((LANES - 8 * OWN_HEADS, HEAD_DIM), jnp.float32))
    stats = jnp.concatenate(stats, axis=0).T
    lane = lane_of(stats.shape)
    for pair in range(2):
        both = outs[pair]
        stat_ref[:, pair, :] = jnp.where(lane < HEAD_DIM, both[:HEAD_DIM], both[HEAD_DIM:]).astype(jnp.bfloat16)
    stat_ref[:, 2, :] = jnp.where(lane < HEAD_DIM, stats, outs[2]).astype(jnp.bfloat16)
    stat_ref[:, 3, :] = jnp.zeros(stats.shape, jnp.bfloat16)
    for store in stores:
        store.wait()


def of_heads(value, left, right):
    shape = value.shape
    return jnp.where(
        lane_of(shape) < HEAD_DIM,
        jnp.broadcast_to(value[..., 8 * left : 8 * left + 1], shape),
        jnp.broadcast_to(value[..., 8 * right : 8 * right + 1], shape),
    )


def combine_kernel(in_ref, done_ref, out_ref, *, sources):
    terms = in_ref[...].astype(jnp.float32)
    rows = [terms[:, row, :] for row in range(3)]
    if sources != terms.shape[0]:
        rows = [row.reshape(sources, -1, LANES) for row in rows]
    added = three_added(rows[2])
    peak = lanes_left(added, 3)
    top = jnp.max(peak, axis=0, keepdims=True)
    weight = jnp.exp(peak - top)
    total = jnp.sum(added * weight, axis=0, keepdims=True)
    heads = ((0, 1), (2, 3), (4, 4))
    outs = []
    for row, pair in zip(rows, heads):
        outs.append(jnp.sum(row * of_heads(weight, *pair), axis=0, keepdims=True) / of_heads(total, *pair))
    lse = top + jnp.log(jnp.where(lane_of(total.shape) % 8 == 0, total, 1.0))
    first, second, third = three_terms(lse)
    kind = lane_of(lse.shape) % 8
    second = jnp.concatenate([second[..., -1:], second[..., :-1]], axis=-1)
    third = jnp.concatenate([third[..., -2:], third[..., :-2]], axis=-1)
    stat = jnp.where(kind == 0, first, jnp.where(kind == 1, second, jnp.where(kind == 2, third, 0.0)))
    outs[2] = jnp.where(lane_of(stat.shape) < HEAD_DIM, stat, outs[2])
    outs.append(jnp.zeros_like(stat))
    for row, out in enumerate(outs):
        out = jnp.broadcast_to(out, rows[0].shape).reshape(out_ref.shape[0], LANES)
        out_ref[:, row, :] = out.astype(jnp.bfloat16)


def backward_kernel(
    core_ref, limit_ref, limit2_ref, to_ref, tp_ref, in_ref, q_ref, d_ref, merged_ref, attended_ref, grad_ref,
    rows_ref, turned_ref, kv_ref, sem, kv_sem, *, block_rows,
):
    half_rows = kv_ref.shape[0] // 2
    step = pl.program_id(0)

    @pl.when(step == 0)
    def _():
        fetches = [
            pltpu.make_async_copy(ref, turned_ref.at[half], sem.at[half]) for half, ref in enumerate((to_ref, tp_ref))
        ]
        places = [pl.ds(half * half_rows, half_rows) for half in range(2)]
        loads = [
            pltpu.make_async_copy(in_ref.at[place, :], kv_ref.at[place, :], kv_sem.at[half])
            for half, place in enumerate(places)
        ]
        for fetch in (*loads, *fetches):
            fetch.start()
        first = core_ref[0] == 0
        d_parts = own_half(d_ref, first)
        q_parts = own_half(q_ref, first)
        sides = [diagonal(pair_diagonal(q_parts[pair]), pair_diagonal(d_parts[pair])) for pair in range(2)]
        d_parts[2] = swap_halves(d_parts[2])
        sides.append(jnp.concatenate([q_parts[2], d_parts[2]], axis=0))
        merged = merged_ref[...].astype(jnp.float32)
        stat = three_added(merged[:, 2, :])
        lane = lane_of(stat.shape)
        for part in range(3):
            block = merged[:, part, :]
            product = d_parts[part].astype(jnp.float32) * block
            left = jnp.sum(jnp.where(lane < HEAD_DIM, product, 0.0), axis=1, keepdims=True)
            right = jnp.sum(jnp.where(lane < HEAD_DIM, 0.0, product), axis=1, keepdims=True)
            if part == 2:
                attended_ref[:, 256:] = swap_halves(block).astype(jnp.bfloat16)
                stat = jnp.where(lane == 33, right, stat)
            else:
                attended_ref[:, part * LANES : (part + 1) * LANES] = block.astype(jnp.bfloat16)
                stat = jnp.where(lane == 16 * part + 1, left, jnp.where(lane == 16 * part + 9, right, stat))
        stat = stat.T

        def row_of(heads, offset):
            return jnp.concatenate([stat[8 * head + offset : 8 * head + offset + 1] for head in heads], axis=1)

        for half, limits in enumerate((limit_ref, limit2_ref)):
            loads[half].wait()
            kv = kv_ref[half * half_rows : (half + 1) * half_rows, :]
            pairs = (
                (jnp.concatenate([kv[:, :128], kv[:, 384:512]], axis=1), (0, 1)),
                (jnp.concatenate([kv[:, 128:256], kv[:, 512:]], axis=1), (2, 3)),
                (kv[:, 256:384], (4,)),
            )
            target = slice(half * half_rows, (half + 1) * half_rows)
            for index, ((pair, heads), side) in enumerate(zip(pairs, sides)):
                span = HEAD_DIM * len(heads)
                both = mm(pair, side, NT)
                probs = jnp.exp(masked(both[:, :span], limits, block_rows) - row_of(heads, 0))
                score_grad = probs * (both[:, span:] - row_of(heads, 1))
                pair = jnp.concatenate([score_grad.astype(jnp.bfloat16), probs.astype(jnp.bfloat16)], axis=1)
                rows = mm(pair, side, NN).astype(jnp.bfloat16)
                if index == 2:
                    rows_ref[target, 256:384] = rows
                else:
                    rows_ref[target, index * LANES : (index + 1) * LANES] = rows[:, :LANES]
                    rows_ref[target, 384 + index * LANES : 512 + index * LANES] = rows[:, LANES:]
        for fetch in fetches:
            fetch.wait()

    size = grad_ref.shape[0]
    part = pl.ds(pl.multiple_of(step * size, size), size)
    grads = mm(turned_ref[0, part, :], rows_ref[:half_rows, :], NN) + mm(turned_ref[1, part, :], rows_ref[half_rows:, :], NN)
    grad_ref[...] = grads.astype(jnp.bfloat16)


def fold_kernel(in_ref, out_ref, *, length, reps):
    total = in_ref[0].astype(jnp.float32)
    for source in range(1, in_ref.shape[0]):
        total = total + in_ref[source].astype(jnp.float32)
    keys = total[:, :HALF]
    values = jnp.concatenate([total[:, 384:], total[:, HALF:384]], axis=1)
    pieces, padded, lanes = out_ref.shape
    width = 2 * HALF // reps
    for local in range(reps // 2):
        cols = slice(local * width, (local + 1) * width)
        part = jnp.concatenate([keys[:, cols], values[:, cols]], axis=1)
        if lanes != part.shape[1]:
            part = jnp.concatenate([part, jnp.zeros((part.shape[0], lanes - part.shape[1]), jnp.float32)], axis=1)
        for block in range(2 * pieces // reps):
            piece = part[block * length : (block + 1) * length]
            if padded != length:
                piece = jnp.concatenate([piece, jnp.zeros((padded - length, lanes), jnp.float32)], axis=0)
            out_ref[block * (reps // 2) + local] = piece.astype(jnp.bfloat16)


def whole(shape):
    return pl.BlockSpec(shape, lambda step, *_: (0,) * len(shape))


def row_block(rows, cols):
    return pl.BlockSpec((rows, cols), lambda step, *_: (step, 0))


def shaped(shape, dtype=jnp.bfloat16):
    return jax.ShapeDtypeStruct(shape, dtype)


def call(kernel, name, scalars, grid, in_specs, out_specs, out_shape, flops, nbytes, scratch=(), vmem=VMEM_LIMIT):
    return pl.pallas_call(
        kernel,
        name=name,
        out_shape=out_shape,
        grid_spec=pltpu.PrefetchScalarGridSpec(
            num_scalar_prefetch=scalars, grid=grid, in_specs=in_specs, out_specs=out_specs, scratch_shapes=scratch
        ),
        compiler_params=pltpu.CompilerParams(dimension_semantics=("arbitrary",), vmem_limit_bytes=vmem),
        cost_estimate=pl.CostEstimate(flops=flops, bytes_accessed=nbytes, transcendentals=0),
    )


def device(z, y, c, x):
    _, ys, cs, xs = GRID
    return ((z * ys + y) * cs + c) * xs + x


def first_groups():
    zs, ys, _, xs = GRID
    groups = []
    for x in range(xs):
        groups += [[device(z, y, 0, x) for z in range(zs)] for y in range(ys)]
        groups += [[device(z, y, 1, x) for y in range(ys)] for z in range(zs)]
    return groups


def second_groups():
    zs, ys, _, xs = GRID
    groups = [[device(z, y, 0, x) for y in range(ys) for x in range(xs)] for z in range(zs)]
    groups += [[device(z, y, 1, x) for z in range(zs) for x in range(xs)] for y in range(ys)]
    return groups


def padded_to(count, unit):
    return -(-count // unit) * unit


def body(tile_embed, block_slide, block_rank, tile_count, queries, w_key, w_value, d_attended):
    zs, ys, _, xs = GRID
    _, slots, block_rows, width_in = tile_embed.shape
    rows = slots * block_rows
    latents, width = queries.shape
    core = lax.axis_index("c")
    first = core == 0
    both_rows = 2 * rows
    big_flops = 2 * both_rows * width_in * width
    core_arg = core.astype(jnp.int32)[None]
    rep_arg = lax.axis_index("x").astype(jnp.int32)[None]
    anywhere = pl.BlockSpec(memory_space=pl.ANY)
    in_vmem = pl.BlockSpec(memory_space=pltpu.VMEM)
    in_hbm = pl.BlockSpec(memory_space=pltpu.HBM)

    def partner(value):
        return lax.ppermute(value, "c", [(0, 1), (1, 0)])

    def shifted(value, by):
        return lax.ppermute(value, "x", [(x, (x + by) % xs) for x in range(xs)])

    key_half = jnp.where(first, w_key[:, :HALF], w_key[:, HALF:])
    value_half = jnp.where(first, w_value[:, :HALF], w_value[:, HALF:])
    w_own = jnp.concatenate([key_half, value_half[:, 256:], value_half[:, :256]], axis=1)
    w_parts = [w_own]
    for _ in range(min(2, xs - 1)):
        w_parts.append(shifted(w_parts[-1], -1))
    if xs == 4:
        w_parts.append(shifted(w_own, 1))
    q_scaled = (queries.astype(jnp.float32) * SCORE_SCALE).astype(jnp.bfloat16)

    x_own = tile_embed.reshape(rows, width_in)
    x_part = partner(x_own)
    limits = jnp.where(block_slide[0] >= 0, tile_count[0, 0] - block_rank[0] * block_rows, 0)
    limits2 = partner(limits)

    def turned(tiles, after, name):
        return call(
            lambda *refs: turn_kernel(*refs, zs=zs, ys=ys), name, 1, (5,), [in_vmem, anywhere],
            (row_block(width_in // 5, rows), whole((8, LANES))), (pltpu.HBM((width_in, rows), jnp.bfloat16), shaped((8, LANES), jnp.float32)),
            2 * rows * width_in * width_in, 5 << 20, (), FORWARD_LIMIT,
        )(core_arg, tiles, after)

    turned_own, own_done = turned(x_own, q_scaled, "turn_own")

    stat_shape = (latents, 4, LANES)
    kv, stats = call(
        lambda *refs: forward_kernel(*refs, block_rows=block_rows, reps=xs), "forward_pass", 4, (1,),
        [in_vmem, in_hbm, *[in_vmem] * xs, in_vmem, in_vmem], (in_hbm, in_vmem),
        (pltpu.HBM((both_rows, width), jnp.bfloat16), shaped(stat_shape)), big_flops, 10 << 20,
        [
            pltpu.VMEM((width_in, width), jnp.bfloat16), pltpu.VMEM((rows, width_in), jnp.bfloat16),
            pltpu.VMEM((both_rows, width), jnp.bfloat16), pltpu.SemaphoreType.DMA((1,)), pltpu.SemaphoreType.DMA((2,)),
        ],
        FORWARD_LIMIT,
    )(core_arg, rep_arg, limits, limits2, x_own, x_part, *w_parts, q_scaled, own_done)

    turned_part, part_done = turned(x_part, stats, "turn_partner")
    chips = ("z", "y")
    stats = lax.all_to_all(stats, chips, 0, 0, tiled=True)
    merged = call(
        lambda *refs: combine_kernel(*refs, sources=zs * ys), "combine", 0, (1,),
        [in_vmem] * 2, in_vmem, shaped(stat_shape), stats.size * 4, stats.size * 4, (), FORWARD_LIMIT,
    )(stats, part_done)
    merged = lax.all_to_all(merged, chips, 0, 0, tiled=True)

    d_out = d_attended.reshape(latents, width)
    turned_own, turned_part = (pltpu.with_memory_space_constraint(part, pltpu.HBM) for part in (turned_own, turned_part))
    kv = pltpu.with_memory_space_constraint(kv, pltpu.HBM)
    attended, grads = call(
        lambda *refs: backward_kernel(*refs, block_rows=block_rows), "backward_pass", 3, (2,),
        [in_hbm, in_hbm, in_hbm, in_vmem, whole(d_out.shape), in_vmem],
        (whole((latents, 3 * LANES)), row_block(width_in // 2, width)),
        (shaped((latents, 3 * LANES)), shaped((width_in, width))),
        big_flops, 10 << 20,
        [
            pltpu.VMEM((both_rows, width), jnp.bfloat16), pltpu.VMEM((2, width_in, rows), jnp.bfloat16),
            pltpu.VMEM((both_rows, width), jnp.bfloat16), pltpu.SemaphoreType.DMA((2,)), pltpu.SemaphoreType.DMA((2,)),
        ],
        BACKWARD_LIMIT,
    )(core_arg, limits, limits2, turned_own, turned_part, kv, q_scaled, d_out, merged)
    mine = attended[:, :HALF]
    theirs = partner(mine)
    attended = jnp.where(first, jnp.concatenate([mine, theirs], axis=1), jnp.concatenate([theirs, mine], axis=1))

    received = lax.all_to_all(grads, AXES, 0, 0, axis_index_groups=first_groups(), tiled=True)
    received = received.reshape(zs, width_in // zs, width)
    length = width_in // (2 * zs * ys)
    share = width // xs
    chunk = (ys * xs, padded_to(length, 16), padded_to(2 * share, LANES))
    pieces = call(
        lambda *refs: fold_kernel(*refs, length=length, reps=xs), "fold", 0, (1,), [whole(received.shape)],
        whole(chunk), shaped(chunk), received.size, received.size * 2, (), FORWARD_LIMIT,
    )(received)
    received = lax.all_to_all(pieces, AXES, 0, 0, axis_index_groups=second_groups(), tiled=True)
    total = jnp.sum(received.astype(jnp.float32), axis=0)[:length, : 2 * share]
    half = xs // 2
    home = [(c * xs + x, (x // half) * xs + c * half + x % half) for c in range(2) for x in range(xs)]
    total = lax.ppermute(total, ("c", "x"), home)
    return (attended.reshape(1, 1, latents, width), total[:, :share], total[:, share:])


def solution(mesh):
    grid = Mesh(mesh.devices.reshape(GRID), AXES)
    placed = (
        P("x", TILES, None, None),
        P("x", TILES),
        P("x", TILES),
        P("x", None),
        P(),
        P("x", None),
        P("x", None),
        P("x", None, None, None),
    )
    return jax.shard_map(
        body,
        mesh=grid,
        in_specs=placed,
        out_specs=(P("x", None, None, None), P(TILES, "x"), P(TILES, "x")),
        check_vma=False,
    )
```

```python
import jax
import jax.numpy as jnp
from jax import lax
from jax.experimental import pallas as pl
from jax.experimental.pallas import tpu as pltpu
from jax.sharding import Mesh, PartitionSpec as P

HEAD_DIM = 64
OWN_HEADS = 5
HALF = OWN_HEADS * HEAD_DIM
LANES = 128
SCORE_SCALE = 0.125
MASKED_SCORE = -1e30

VMEM_LIMIT = 59 << 20
FORWARD_LIMIT = 32 << 20
BACKWARD_LIMIT = 48 << 20

GRID = (8, 8, 2, 4)
AXES = ("z", "y", "c", "x")
TILES = ("z", "y", "c")

NT = (((1,), (1,)), ((), ()))
TN = (((0,), (0,)), ((), ()))
NN = (((1,), (0,)), ((), ()))


def mm(one, two, dims):
    return lax.dot_general(one, two, dims, preferred_element_type=jnp.float32)


def lane_of(shape):
    return lax.broadcasted_iota(jnp.int32, shape, len(shape) - 1)


def swap_halves(part):
    return jnp.concatenate([part[:, HEAD_DIM:], part[:, :HEAD_DIM]], axis=1)


def pair_diagonal(part):
    lane = lane_of(part.shape)
    zero = jnp.zeros_like(part)
    return jnp.concatenate([jnp.where(lane < HEAD_DIM, part, zero), jnp.where(lane < HEAD_DIM, zero, part)], axis=0)


def own_half(ref, first):
    full = ref[...].astype(jnp.float32)
    part = jnp.where(first, full[:, :HALF], full[:, HALF:])
    last = jnp.concatenate([part[:, 256:], jnp.zeros_like(part[:, 256:])], axis=1)
    return [piece.astype(jnp.bfloat16) for piece in (part[:, :128], part[:, 128:256], last)]


def diagonal(one, two):
    right = jnp.zeros((one.shape[0], two.shape[1]), one.dtype)
    below = jnp.zeros((two.shape[0], one.shape[1]), one.dtype)
    return jnp.concatenate([jnp.concatenate([one, right], axis=1), jnp.concatenate([below, two], axis=1)], axis=0)


def masked(scores, limit_ref, block_rows):
    pieces = []
    for block in range(scores.shape[0] // block_rows):
        piece = scores[block * block_rows : (block + 1) * block_rows]
        row = lax.broadcasted_iota(jnp.int32, piece.shape, 0)
        pieces.append(jnp.where(row < limit_ref[block], piece, MASKED_SCORE))
    return jnp.concatenate(pieces, axis=0)


def turn_kernel(core_ref, x_ref, after_ref, out_ref, token_ref, *, zs, ys):
    rows, unit = out_ref.shape[0], x_ref.shape[1] // (zs * ys)
    row = lax.broadcasted_iota(jnp.int32, (rows, 1), 0) + pl.program_id(0) * rows
    middle = row.astype(jnp.float32) + 0.5
    outer = (middle * (1.0 / (zs * unit))).astype(jnp.int32)
    piece = (middle * (1.0 / unit)).astype(jnp.int32)
    by_y = ((piece - outer * zs) * ys + outer) * unit + row - piece * unit
    source = jnp.where(core_ref[0] == 0, row, by_y)
    chosen = lane_of((rows, x_ref.shape[1])) == source
    out_ref[...] = mm(jnp.where(chosen, 1.0, 0.0).astype(jnp.bfloat16), x_ref[...], NT).astype(jnp.bfloat16)
    token_ref[...] = jnp.zeros_like(token_ref)


def three_terms(value):
    terms = []
    for _ in range(3):
        term = value.astype(jnp.bfloat16).astype(jnp.float32)
        terms.append(term)
        value = value - term
    return terms


def lanes_left(value, by):
    return jnp.concatenate([value[..., by:], value[..., :by]], axis=-1)


def three_added(value):
    return value + lanes_left(value, 1) + lanes_left(value, 2)


def forward_kernel(
    core_ref, rep_ref, limit_ref, limit2_ref, xo_ref, xp_ref, *refs, block_rows, reps
):
    part_refs = refs[:reps]
    q_ref, _, kv_ref, stat_ref, w_ref, held_ref, sem = refs[reps:]
    share = part_refs[0].shape[0]
    rows = xo_ref.shape[0]
    fetch = pltpu.make_async_copy(xp_ref, held_ref, sem.at[0])
    fetch.start()
    for index, part in enumerate(part_refs):
        origin = (rep_ref[0] + index) % reps
        w_ref[pl.ds(pl.multiple_of(origin * share, share), share), :] = part[...]
    q_parts = own_half(q_ref, core_ref[0] == 0)
    wide = diagonal(pair_diagonal(q_parts[0]), pair_diagonal(q_parts[1]))
    scores, last_scores = [], []
    for half, (x_ref, limits) in enumerate(((xo_ref, limit_ref), (held_ref, limit2_ref))):
        if half == 1:
            fetch.wait()
        kv = mm(x_ref[...], w_ref[...], NN).astype(jnp.bfloat16)
        kv_ref[half * rows : (half + 1) * rows, :] = kv
        scores.append(masked(mm(kv[:, :256], wide, NT), limits, block_rows))
        last_scores.append(masked(mm(kv[:, 256:384], q_parts[2], NT), limits, block_rows))
    outs, stats = [], []
    for parts, columns in ((scores, (384, 512)), (last_scores, (256,))):
        peak = jnp.maximum(*[jnp.max(part, axis=0, keepdims=True) for part in parts])
        total = jnp.zeros_like(peak)
        sums = [0.0] * len(columns)
        for half, part in enumerate(parts):
            p = jnp.exp(part - peak)
            total = total + jnp.sum(p, axis=0, keepdims=True)
            p = p.astype(jnp.bfloat16)
            span = p.shape[1] // len(columns)
            for index, column in enumerate(columns):
                values = kv_ref[half * rows : (half + 1) * rows, column : column + LANES]
                sums[index] = sums[index] + mm(p[:, index * span : (index + 1) * span], values, TN)
        outs += sums
        for head in range(peak.shape[1] // HEAD_DIM):
            cols = slice(head * HEAD_DIM, (head + 1) * HEAD_DIM)
            pad = jnp.zeros((2, HEAD_DIM), jnp.float32)
            stats.append(jnp.concatenate([*three_terms(total[:, cols]), *three_terms(peak[:, cols]), pad], axis=0))
    stats.append(jnp.zeros((LANES - 8 * OWN_HEADS, HEAD_DIM), jnp.float32))
    stats = jnp.concatenate(stats, axis=0).T
    lane = lane_of(stats.shape)
    for pair in range(2):
        both = outs[pair]
        stat_ref[:, 0, pair * LANES : (pair + 1) * LANES] = jnp.where(lane < HEAD_DIM, both[:HEAD_DIM], both[HEAD_DIM:])
    stat_ref[:, 0, 2 * LANES :] = jnp.where(lane < HEAD_DIM, stats, outs[2])


def of_heads(value, left, right):
    shape = value.shape
    return jnp.where(
        lane_of(shape) < HEAD_DIM,
        jnp.broadcast_to(value[..., 8 * left : 8 * left + 1], shape),
        jnp.broadcast_to(value[..., 8 * right : 8 * right + 1], shape),
    )


def combine_kernel(in_ref, done_ref, out_ref, *, sources):
    rows = [in_ref[:, 0, row * LANES : (row + 1) * LANES] for row in range(3)]
    if sources != in_ref.shape[0]:
        rows = [row.reshape(sources, -1, LANES) for row in rows]
    added = three_added(rows[2])
    peak = lanes_left(added, 3)
    top = jnp.max(peak, axis=0, keepdims=True)
    weight = jnp.exp(peak - top)
    total = jnp.sum(added * weight, axis=0, keepdims=True)
    heads = ((0, 1), (2, 3), (4, 4))
    outs = []
    for row, pair in zip(rows, heads):
        outs.append(jnp.sum(row * of_heads(weight, *pair), axis=0, keepdims=True) / of_heads(total, *pair))
    lse = top + jnp.log(jnp.where(lane_of(total.shape) % 8 == 0, total, 1.0))
    first, second, third = three_terms(lse)
    kind = lane_of(lse.shape) % 8
    second = jnp.concatenate([second[..., -1:], second[..., :-1]], axis=-1)
    third = jnp.concatenate([third[..., -2:], third[..., :-2]], axis=-1)
    stat = jnp.where(kind == 0, first, jnp.where(kind == 1, second, jnp.where(kind == 2, third, 0.0)))
    outs[2] = jnp.where(lane_of(stat.shape) < HEAD_DIM, stat, outs[2])
    for row, out in enumerate(outs):
        if row < 2:
            out = out.astype(jnp.bfloat16).astype(jnp.float32)
        else:
            out = jnp.where(lane_of(out.shape) < HEAD_DIM, out, out.astype(jnp.bfloat16).astype(jnp.float32))
        out = jnp.broadcast_to(out, rows[0].shape).reshape(out_ref.shape[0], LANES)
        out_ref[:, 0, row * LANES : (row + 1) * LANES] = out


def backward_kernel(
    core_ref, limit_ref, limit2_ref, to_ref, tp_ref, kv_ref, q_ref, d_ref, merged_ref, attended_ref, grad_ref,
    rows_ref, turned_ref, sem, *, block_rows,
):
    half_rows = kv_ref.shape[0] // 2
    step = pl.program_id(0)

    @pl.when(step == 0)
    def _():
        fetches = [
            pltpu.make_async_copy(ref, turned_ref.at[half], sem.at[half]) for half, ref in enumerate((to_ref, tp_ref))
        ]
        for fetch in fetches:
            fetch.start()
        first = core_ref[0] == 0
        d_parts = own_half(d_ref, first)
        q_parts = own_half(q_ref, first)
        sides = [diagonal(pair_diagonal(q_parts[pair]), pair_diagonal(d_parts[pair])) for pair in range(2)]
        d_parts[2] = swap_halves(d_parts[2])
        sides.append(jnp.concatenate([q_parts[2], d_parts[2]], axis=0))
        stat = three_added(merged_ref[:, 0, 2 * LANES :])
        lane = lane_of(stat.shape)
        for part in range(3):
            block = merged_ref[:, 0, part * LANES : (part + 1) * LANES]
            product = d_parts[part].astype(jnp.float32) * block
            left = jnp.sum(jnp.where(lane < HEAD_DIM, product, 0.0), axis=1, keepdims=True)
            right = jnp.sum(jnp.where(lane < HEAD_DIM, 0.0, product), axis=1, keepdims=True)
            if part == 2:
                attended_ref[:, 256:] = swap_halves(block).astype(jnp.bfloat16)
                stat = jnp.where(lane == 33, right, stat)
            else:
                attended_ref[:, part * LANES : (part + 1) * LANES] = block.astype(jnp.bfloat16)
                stat = jnp.where(lane == 16 * part + 1, left, jnp.where(lane == 16 * part + 9, right, stat))
        stat = stat.T

        def row_of(heads, offset):
            return jnp.concatenate([stat[8 * head + offset : 8 * head + offset + 1] for head in heads], axis=1)

        for half, limits in enumerate((limit_ref, limit2_ref)):
            kv = kv_ref[half * half_rows : (half + 1) * half_rows, :]
            pairs = (
                (jnp.concatenate([kv[:, :128], kv[:, 384:512]], axis=1), (0, 1)),
                (jnp.concatenate([kv[:, 128:256], kv[:, 512:]], axis=1), (2, 3)),
                (kv[:, 256:384], (4,)),
            )
            target = slice(half * half_rows, (half + 1) * half_rows)
            for index, ((pair, heads), side) in enumerate(zip(pairs, sides)):
                span = HEAD_DIM * len(heads)
                both = mm(pair, side, NT)
                probs = jnp.exp(masked(both[:, :span], limits, block_rows) - row_of(heads, 0))
                score_grad = probs * (both[:, span:] - row_of(heads, 1))
                pair = jnp.concatenate([score_grad.astype(jnp.bfloat16), probs.astype(jnp.bfloat16)], axis=1)
                rows = mm(pair, side, NN).astype(jnp.bfloat16)
                if index == 2:
                    rows_ref[target, 256:384] = rows
                else:
                    rows_ref[target, index * LANES : (index + 1) * LANES] = rows[:, :LANES]
                    rows_ref[target, 384 + index * LANES : 512 + index * LANES] = rows[:, LANES:]
        for fetch in fetches:
            fetch.wait()

    size = grad_ref.shape[0]
    part = pl.ds(pl.multiple_of(step * size, size), size)
    grads = mm(turned_ref[0, part, :], rows_ref[:half_rows, :], NN) + mm(turned_ref[1, part, :], rows_ref[half_rows:, :], NN)
    grad_ref[...] = grads.astype(jnp.bfloat16)


def fold_kernel(in_ref, out_ref, *, length, reps):
    total = in_ref[0].astype(jnp.float32)
    for source in range(1, in_ref.shape[0]):
        total = total + in_ref[source].astype(jnp.float32)
    keys = total[:, :HALF]
    values = jnp.concatenate([total[:, 384:], total[:, HALF:384]], axis=1)
    pieces, padded, lanes = out_ref.shape
    width = 2 * HALF // reps
    for local in range(reps // 2):
        cols = slice(local * width, (local + 1) * width)
        part = jnp.concatenate([keys[:, cols], values[:, cols]], axis=1)
        if lanes != part.shape[1]:
            part = jnp.concatenate([part, jnp.zeros((part.shape[0], lanes - part.shape[1]), jnp.float32)], axis=1)
        for block in range(2 * pieces // reps):
            piece = part[block * length : (block + 1) * length]
            if padded != length:
                piece = jnp.concatenate([piece, jnp.zeros((padded - length, lanes), jnp.float32)], axis=0)
            out_ref[block * (reps // 2) + local] = piece.astype(jnp.bfloat16)


def whole(shape):
    return pl.BlockSpec(shape, lambda step, *_: (0,) * len(shape))


def row_block(rows, cols):
    return pl.BlockSpec((rows, cols), lambda step, *_: (step, 0))


def shaped(shape, dtype=jnp.bfloat16):
    return jax.ShapeDtypeStruct(shape, dtype)


def call(kernel, name, scalars, grid, in_specs, out_specs, out_shape, flops, nbytes, scratch=(), vmem=VMEM_LIMIT):
    return pl.pallas_call(
        kernel,
        name=name,
        out_shape=out_shape,
        grid_spec=pltpu.PrefetchScalarGridSpec(
            num_scalar_prefetch=scalars, grid=grid, in_specs=in_specs, out_specs=out_specs, scratch_shapes=scratch
        ),
        compiler_params=pltpu.CompilerParams(dimension_semantics=("arbitrary",), vmem_limit_bytes=vmem),
        cost_estimate=pl.CostEstimate(flops=flops, bytes_accessed=nbytes, transcendentals=0),
    )


def device(z, y, c, x):
    _, ys, cs, xs = GRID
    return ((z * ys + y) * cs + c) * xs + x


def first_groups():
    zs, ys, _, xs = GRID
    groups = []
    for x in range(xs):
        groups += [[device(z, y, 0, x) for z in range(zs)] for y in range(ys)]
        groups += [[device(z, y, 1, x) for y in range(ys)] for z in range(zs)]
    return groups


def second_groups():
    zs, ys, _, xs = GRID
    groups = [[device(z, y, 0, x) for y in range(ys) for x in range(xs)] for z in range(zs)]
    groups += [[device(z, y, 1, x) for z in range(zs) for x in range(xs)] for y in range(ys)]
    return groups


def padded_to(count, unit):
    return -(-count // unit) * unit


def body(tile_embed, block_slide, block_rank, tile_count, queries, w_key, w_value, d_attended):
    zs, ys, _, xs = GRID
    _, slots, block_rows, width_in = tile_embed.shape
    rows = slots * block_rows
    latents, width = queries.shape
    core = lax.axis_index("c")
    first = core == 0
    both_rows = 2 * rows
    big_flops = 2 * both_rows * width_in * width
    core_arg = core.astype(jnp.int32)[None]
    rep_arg = lax.axis_index("x").astype(jnp.int32)[None]
    anywhere = pl.BlockSpec(memory_space=pl.ANY)
    in_vmem = pl.BlockSpec(memory_space=pltpu.VMEM)
    in_hbm = pl.BlockSpec(memory_space=pltpu.HBM)

    def partner(value):
        return lax.ppermute(value, "c", [(0, 1), (1, 0)])

    def shifted(value, by):
        return lax.ppermute(value, "x", [(x, (x + by) % xs) for x in range(xs)])

    key_half = jnp.where(first, w_key[:, :HALF], w_key[:, HALF:])
    value_half = jnp.where(first, w_value[:, :HALF], w_value[:, HALF:])
    w_own = jnp.concatenate([key_half, value_half[:, 256:], value_half[:, :256]], axis=1)
    w_parts = [w_own]
    for _ in range(min(2, xs - 1)):
        w_parts.append(shifted(w_parts[-1], -1))
    if xs == 4:
        w_parts.append(shifted(w_own, 1))
    q_scaled = (queries.astype(jnp.float32) * SCORE_SCALE).astype(jnp.bfloat16)

    x_own = tile_embed.reshape(rows, width_in)
    x_part = partner(x_own)
    limits = jnp.where(block_slide[0] >= 0, tile_count[0, 0] - block_rank[0] * block_rows, 0)
    limits2 = partner(limits)

    def turned(tiles, after, name):
        return call(
            lambda *refs: turn_kernel(*refs, zs=zs, ys=ys), name, 1, (5,), [in_vmem, anywhere],
            (row_block(width_in // 5, rows), whole((8, LANES))), (pltpu.HBM((width_in, rows), jnp.bfloat16), shaped((8, LANES), jnp.float32)),
            2 * rows * width_in * width_in, 5 << 20, (), FORWARD_LIMIT,
        )(core_arg, tiles, after)

    turned_own, own_done = turned(x_own, q_scaled, "turn_own")

    stat_shape = (latents, 1, 3 * LANES)
    kv, stats = call(
        lambda *refs: forward_kernel(*refs, block_rows=block_rows, reps=xs), "forward_pass", 4, (1,),
        [in_vmem, in_hbm, *[in_vmem] * xs, in_vmem, in_vmem], (in_vmem, in_vmem),
        (shaped((both_rows, width)), shaped(stat_shape, jnp.float32)), big_flops, 10 << 20,
        [
            pltpu.VMEM((width_in, width), jnp.bfloat16), pltpu.VMEM((rows, width_in), jnp.bfloat16),
            pltpu.SemaphoreType.DMA((1,)),
        ],
        FORWARD_LIMIT,
    )(core_arg, rep_arg, limits, limits2, x_own, x_part, *w_parts, q_scaled, own_done)

    turned_part, part_done = turned(x_part, stats, "turn_partner")
    chips = ("z", "y")
    stats = lax.all_to_all(stats, chips, 0, 0, tiled=True)
    merged = call(
        lambda *refs: combine_kernel(*refs, sources=zs * ys), "combine", 0, (1,),
        [in_vmem] * 2, in_vmem, shaped(stat_shape, jnp.float32), stats.size * 4, stats.size * 4, (), FORWARD_LIMIT,
    )(stats, part_done)
    merged = lax.all_to_all(merged, chips, 0, 0, tiled=True)

    d_out = d_attended.reshape(latents, width)
    turned_own, turned_part = (pltpu.with_memory_space_constraint(part, pltpu.HBM) for part in (turned_own, turned_part))
    attended, grads = call(
        lambda *refs: backward_kernel(*refs, block_rows=block_rows), "backward_pass", 3, (2,),
        [in_hbm, in_hbm, in_vmem, in_vmem, whole(d_out.shape), in_vmem],
        (whole((latents, 3 * LANES)), row_block(width_in // 2, width)),
        (shaped((latents, 3 * LANES)), shaped((width_in, width))),
        big_flops, 10 << 20,
        [
            pltpu.VMEM((both_rows, width), jnp.bfloat16), pltpu.VMEM((2, width_in, rows), jnp.bfloat16),
            pltpu.SemaphoreType.DMA((2,)),
        ],
        BACKWARD_LIMIT,
    )(core_arg, limits, limits2, turned_own, turned_part, kv, q_scaled, d_out, merged)
    mine = attended[:, :HALF]
    theirs = partner(mine)
    attended = jnp.where(first, jnp.concatenate([mine, theirs], axis=1), jnp.concatenate([theirs, mine], axis=1))

    received = lax.all_to_all(grads, AXES, 0, 0, axis_index_groups=first_groups(), tiled=True)
    received = received.reshape(zs, width_in // zs, width)
    length = width_in // (2 * zs * ys)
    share = width // xs
    chunk = (ys * xs, padded_to(length, 16), padded_to(2 * share, LANES))
    pieces = call(
        lambda *refs: fold_kernel(*refs, length=length, reps=xs), "fold", 0, (1,), [whole(received.shape)],
        whole(chunk), shaped(chunk), received.size, received.size * 2, (), FORWARD_LIMIT,
    )(received)
    received = lax.all_to_all(pieces, AXES, 0, 0, axis_index_groups=second_groups(), tiled=True)
    total = jnp.sum(received.astype(jnp.float32), axis=0)[:length, : 2 * share]
    half = xs // 2
    home = [(c * xs + x, (x // half) * xs + c * half + x % half) for c in range(2) for x in range(xs)]
    total = lax.ppermute(total, ("c", "x"), home)
    return (attended.reshape(1, 1, latents, width), total[:, :share], total[:, share:])


def solution(mesh):
    grid = Mesh(mesh.devices.reshape(GRID), AXES)
    placed = (
        P("x", TILES, None, None),
        P("x", TILES),
        P("x", TILES),
        P("x", None),
        P(),
        P("x", None),
        P("x", None),
        P("x", None, None, None),
    )
    return jax.shard_map(
        body,
        mesh=grid,
        in_specs=placed,
        out_specs=(P("x", None, None, None), P(TILES, "x"), P(TILES, "x")),
        check_vma=False,
    )
```

```python
import jax
import jax.numpy as jnp
from jax import lax
from jax.experimental import pallas as pl
from jax.experimental.pallas import tpu as pltpu
from jax.sharding import Mesh, PartitionSpec as P

HEAD_DIM = 64
OWN_HEADS = 5
HALF = OWN_HEADS * HEAD_DIM
LANES = 128
SCORE_SCALE = 0.125
MASKED_SCORE = -1e30

VMEM_LIMIT = 59 << 20
FORWARD_LIMIT = 32 << 20
BACKWARD_LIMIT = 48 << 20

GRID = (8, 8, 2, 4)
AXES = ("z", "y", "c", "x")
TILES = ("z", "y", "c")

NT = (((1,), (1,)), ((), ()))
TN = (((0,), (0,)), ((), ()))
NN = (((1,), (0,)), ((), ()))


def mm(one, two, dims):
    return lax.dot_general(one, two, dims, preferred_element_type=jnp.float32)


def lane_of(shape):
    return lax.broadcasted_iota(jnp.int32, shape, len(shape) - 1)


def swap_halves(part):
    return jnp.concatenate([part[:, HEAD_DIM:], part[:, :HEAD_DIM]], axis=1)


def pair_diagonal(part):
    lane = lane_of(part.shape)
    zero = jnp.zeros_like(part)
    return jnp.concatenate([jnp.where(lane < HEAD_DIM, part, zero), jnp.where(lane < HEAD_DIM, zero, part)], axis=0)


def own_half(ref, first):
    full = ref[...].astype(jnp.float32)
    part = jnp.where(first, full[:, :HALF], full[:, HALF:])
    last = jnp.concatenate([part[:, 256:], jnp.zeros_like(part[:, 256:])], axis=1)
    return [piece.astype(jnp.bfloat16) for piece in (part[:, :128], part[:, 128:256], last)]


def diagonal(one, two):
    right = jnp.zeros((one.shape[0], two.shape[1]), one.dtype)
    below = jnp.zeros((two.shape[0], one.shape[1]), one.dtype)
    return jnp.concatenate([jnp.concatenate([one, right], axis=1), jnp.concatenate([below, two], axis=1)], axis=0)


def masked(scores, limit_ref, block_rows):
    pieces = []
    for block in range(scores.shape[0] // block_rows):
        piece = scores[block * block_rows : (block + 1) * block_rows]
        row = lax.broadcasted_iota(jnp.int32, piece.shape, 0)
        pieces.append(jnp.where(row < limit_ref[block], piece, MASKED_SCORE))
    return jnp.concatenate(pieces, axis=0)


def turn_kernel(core_ref, x_ref, after_ref, out_ref, token_ref, *, zs, ys):
    rows, unit = out_ref.shape[0], x_ref.shape[1] // (zs * ys)
    row = lax.broadcasted_iota(jnp.int32, (rows, 1), 0) + pl.program_id(0) * rows
    middle = row.astype(jnp.float32) + 0.5
    outer = (middle * (1.0 / (zs * unit))).astype(jnp.int32)
    piece = (middle * (1.0 / unit)).astype(jnp.int32)
    by_y = ((piece - outer * zs) * ys + outer) * unit + row - piece * unit
    source = jnp.where(core_ref[0] == 0, row, by_y)
    chosen = lane_of((rows, x_ref.shape[1])) == source
    out_ref[...] = mm(jnp.where(chosen, 1.0, 0.0).astype(jnp.bfloat16), x_ref[...], NT).astype(jnp.bfloat16)
    token_ref[...] = jnp.zeros_like(token_ref)


def three_terms(value):
    terms = []
    for _ in range(3):
        term = value.astype(jnp.bfloat16).astype(jnp.float32)
        terms.append(term)
        value = value - term
    return terms


def lanes_left(value, by):
    return jnp.concatenate([value[..., by:], value[..., :by]], axis=-1)


def three_added(value):
    return value + lanes_left(value, 1) + lanes_left(value, 2)


def forward_kernel(
    core_ref, rep_ref, limit_ref, limit2_ref, xo_ref, xp_ref, *refs, block_rows, reps
):
    part_refs = refs[:reps]
    q_ref, _, kv_ref, stat_ref, w_ref, held_ref, sem = refs[reps:]
    share = part_refs[0].shape[0]
    rows = xo_ref.shape[0]
    fetch = pltpu.make_async_copy(xp_ref, held_ref, sem.at[0])
    fetch.start()
    for index, part in enumerate(part_refs):
        origin = (rep_ref[0] + index) % reps
        w_ref[pl.ds(pl.multiple_of(origin * share, share), share), :] = part[...]
    q_parts = own_half(q_ref, core_ref[0] == 0)
    wide = diagonal(pair_diagonal(q_parts[0]), pair_diagonal(q_parts[1]))
    scores, last_scores = [], []
    for half, (x_ref, limits) in enumerate(((xo_ref, limit_ref), (held_ref, limit2_ref))):
        if half == 1:
            fetch.wait()
        kv = mm(x_ref[...], w_ref[...], NN).astype(jnp.bfloat16)
        kv_ref[half * rows : (half + 1) * rows, :] = kv
        scores.append(masked(mm(kv[:, :256], wide, NT), limits, block_rows))
        last_scores.append(masked(mm(kv[:, 256:384], q_parts[2], NT), limits, block_rows))
    outs, stats = [], []
    for parts, columns in ((scores, (384, 512)), (last_scores, (256,))):
        peak = jnp.maximum(*[jnp.max(part, axis=0, keepdims=True) for part in parts])
        total = jnp.zeros_like(peak)
        sums = [0.0] * len(columns)
        for half, part in enumerate(parts):
            p = jnp.exp(part - peak)
            total = total + jnp.sum(p, axis=0, keepdims=True)
            p = p.astype(jnp.bfloat16)
            span = p.shape[1] // len(columns)
            for index, column in enumerate(columns):
                values = kv_ref[half * rows : (half + 1) * rows, column : column + LANES]
                sums[index] = sums[index] + mm(p[:, index * span : (index + 1) * span], values, TN)
        outs += sums
        for head in range(peak.shape[1] // HEAD_DIM):
            cols = slice(head * HEAD_DIM, (head + 1) * HEAD_DIM)
            pad = jnp.zeros((2, HEAD_DIM), jnp.float32)
            stats.append(jnp.concatenate([*three_terms(total[:, cols]), *three_terms(peak[:, cols]), pad], axis=0))
    stats.append(jnp.zeros((LANES - 8 * OWN_HEADS, HEAD_DIM), jnp.float32))
    stats = jnp.concatenate(stats, axis=0).T
    lane = lane_of(stats.shape)
    for pair in range(2):
        both = outs[pair]
        stat_ref[:, 0, pair * LANES : (pair + 1) * LANES] = jnp.where(lane < HEAD_DIM, both[:HEAD_DIM], both[HEAD_DIM:])
    stat_ref[:, 0, 2 * LANES :] = jnp.where(lane < HEAD_DIM, stats, outs[2])


def of_heads(value, left, right):
    shape = value.shape
    return jnp.where(
        lane_of(shape) < HEAD_DIM,
        jnp.broadcast_to(value[..., 8 * left : 8 * left + 1], shape),
        jnp.broadcast_to(value[..., 8 * right : 8 * right + 1], shape),
    )


def combine_kernel(in_ref, out_ref, *, sources):
    rows = [in_ref[:, 0, row * LANES : (row + 1) * LANES] for row in range(3)]
    if sources != in_ref.shape[0]:
        rows = [row.reshape(sources, -1, LANES) for row in rows]
    added = three_added(rows[2])
    peak = lanes_left(added, 3)
    top = jnp.max(peak, axis=0, keepdims=True)
    weight = jnp.exp(peak - top)
    total = jnp.sum(added * weight, axis=0, keepdims=True)
    heads = ((0, 1), (2, 3), (4, 4))
    outs = []
    for row, pair in zip(rows, heads):
        outs.append(jnp.sum(row * of_heads(weight, *pair), axis=0, keepdims=True) / of_heads(total, *pair))
    lse = top + jnp.log(jnp.where(lane_of(total.shape) % 8 == 0, total, 1.0))
    first, second, third = three_terms(lse)
    kind = lane_of(lse.shape) % 8
    second = jnp.concatenate([second[..., -1:], second[..., :-1]], axis=-1)
    third = jnp.concatenate([third[..., -2:], third[..., :-2]], axis=-1)
    stat = jnp.where(kind == 0, first, jnp.where(kind == 1, second, jnp.where(kind == 2, third, 0.0)))
    outs[2] = jnp.where(lane_of(stat.shape) < HEAD_DIM, stat, outs[2])
    for row, out in enumerate(outs):
        if row < 2:
            out = out.astype(jnp.bfloat16).astype(jnp.float32)
        else:
            out = jnp.where(lane_of(out.shape) < HEAD_DIM, out, out.astype(jnp.bfloat16).astype(jnp.float32))
        out = jnp.broadcast_to(out, rows[0].shape).reshape(out_ref.shape[0], LANES)
        out_ref[:, 0, row * LANES : (row + 1) * LANES] = out


def backward_kernel(
    core_ref, limit_ref, limit2_ref, to_ref, tp_ref, kv_ref, q_ref, d_ref, merged_ref, attended_ref, grad_ref,
    rows_ref, turned_ref, sem, *, block_rows,
):
    half_rows = kv_ref.shape[0] // 2
    step = pl.program_id(0)

    @pl.when(step == 0)
    def _():
        fetches = [
            pltpu.make_async_copy(ref, turned_ref.at[half], sem.at[half]) for half, ref in enumerate((to_ref, tp_ref))
        ]
        for fetch in fetches:
            fetch.start()
        first = core_ref[0] == 0
        d_parts = own_half(d_ref, first)
        q_parts = own_half(q_ref, first)
        sides = [diagonal(pair_diagonal(q_parts[pair]), pair_diagonal(d_parts[pair])) for pair in range(2)]
        d_parts[2] = swap_halves(d_parts[2])
        sides.append(jnp.concatenate([q_parts[2], d_parts[2]], axis=0))
        stat = three_added(merged_ref[:, 0, 2 * LANES :])
        lane = lane_of(stat.shape)
        for part in range(3):
            block = merged_ref[:, 0, part * LANES : (part + 1) * LANES]
            product = d_parts[part].astype(jnp.float32) * block
            left = jnp.sum(jnp.where(lane < HEAD_DIM, product, 0.0), axis=1, keepdims=True)
            right = jnp.sum(jnp.where(lane < HEAD_DIM, 0.0, product), axis=1, keepdims=True)
            if part == 2:
                attended_ref[:, 256:] = swap_halves(block).astype(jnp.bfloat16)
                stat = jnp.where(lane == 33, right, stat)
            else:
                attended_ref[:, part * LANES : (part + 1) * LANES] = block.astype(jnp.bfloat16)
                stat = jnp.where(lane == 16 * part + 1, left, jnp.where(lane == 16 * part + 9, right, stat))
        stat = stat.T

        def row_of(heads, offset):
            return jnp.concatenate([stat[8 * head + offset : 8 * head + offset + 1] for head in heads], axis=1)

        for half, limits in enumerate((limit_ref, limit2_ref)):
            kv = kv_ref[half * half_rows : (half + 1) * half_rows, :]
            pairs = (
                (jnp.concatenate([kv[:, :128], kv[:, 384:512]], axis=1), (0, 1)),
                (jnp.concatenate([kv[:, 128:256], kv[:, 512:]], axis=1), (2, 3)),
                (kv[:, 256:384], (4,)),
            )
            target = slice(half * half_rows, (half + 1) * half_rows)
            for index, ((pair, heads), side) in enumerate(zip(pairs, sides)):
                span = HEAD_DIM * len(heads)
                both = mm(pair, side, NT)
                probs = jnp.exp(masked(both[:, :span], limits, block_rows) - row_of(heads, 0))
                score_grad = probs * (both[:, span:] - row_of(heads, 1))
                pair = jnp.concatenate([score_grad.astype(jnp.bfloat16), probs.astype(jnp.bfloat16)], axis=1)
                rows = mm(pair, side, NN).astype(jnp.bfloat16)
                if index == 2:
                    rows_ref[target, 256:384] = rows
                else:
                    rows_ref[target, index * LANES : (index + 1) * LANES] = rows[:, :LANES]
                    rows_ref[target, 384 + index * LANES : 512 + index * LANES] = rows[:, LANES:]
        for fetch in fetches:
            fetch.wait()

    size = grad_ref.shape[0]
    part = pl.ds(pl.multiple_of(step * size, size), size)
    grads = mm(turned_ref[0, part, :], rows_ref[:half_rows, :], NN) + mm(turned_ref[1, part, :], rows_ref[half_rows:, :], NN)
    grad_ref[...] = grads.astype(jnp.bfloat16)


def fold_kernel(in_ref, out_ref, *, length, reps):
    total = in_ref[0].astype(jnp.float32)
    for source in range(1, in_ref.shape[0]):
        total = total + in_ref[source].astype(jnp.float32)
    keys = total[:, :HALF]
    values = jnp.concatenate([total[:, 384:], total[:, HALF:384]], axis=1)
    pieces, padded, lanes = out_ref.shape
    width = 2 * HALF // reps
    for local in range(reps // 2):
        cols = slice(local * width, (local + 1) * width)
        part = jnp.concatenate([keys[:, cols], values[:, cols]], axis=1)
        if lanes != part.shape[1]:
            part = jnp.concatenate([part, jnp.zeros((part.shape[0], lanes - part.shape[1]), jnp.float32)], axis=1)
        for block in range(2 * pieces // reps):
            piece = part[block * length : (block + 1) * length]
            if padded != length:
                piece = jnp.concatenate([piece, jnp.zeros((padded - length, lanes), jnp.float32)], axis=0)
            out_ref[block * (reps // 2) + local] = piece.astype(jnp.bfloat16)


def whole(shape):
    return pl.BlockSpec(shape, lambda step, *_: (0,) * len(shape))


def row_block(rows, cols):
    return pl.BlockSpec((rows, cols), lambda step, *_: (step, 0))


def shaped(shape, dtype=jnp.bfloat16):
    return jax.ShapeDtypeStruct(shape, dtype)


def call(kernel, name, scalars, grid, in_specs, out_specs, out_shape, flops, nbytes, scratch=(), vmem=VMEM_LIMIT):
    return pl.pallas_call(
        kernel,
        name=name,
        out_shape=out_shape,
        grid_spec=pltpu.PrefetchScalarGridSpec(
            num_scalar_prefetch=scalars, grid=grid, in_specs=in_specs, out_specs=out_specs, scratch_shapes=scratch
        ),
        compiler_params=pltpu.CompilerParams(dimension_semantics=("arbitrary",), vmem_limit_bytes=vmem),
        cost_estimate=pl.CostEstimate(flops=flops, bytes_accessed=nbytes, transcendentals=0),
    )


def device(z, y, c, x):
    _, ys, cs, xs = GRID
    return ((z * ys + y) * cs + c) * xs + x


def first_groups():
    zs, ys, _, xs = GRID
    groups = []
    for x in range(xs):
        groups += [[device(z, y, 0, x) for z in range(zs)] for y in range(ys)]
        groups += [[device(z, y, 1, x) for y in range(ys)] for z in range(zs)]
    return groups


def second_groups():
    zs, ys, _, xs = GRID
    groups = [[device(z, y, 0, x) for y in range(ys) for x in range(xs)] for z in range(zs)]
    groups += [[device(z, y, 1, x) for z in range(zs) for x in range(xs)] for y in range(ys)]
    return groups


def padded_to(count, unit):
    return -(-count // unit) * unit


def body(tile_embed, block_slide, block_rank, tile_count, queries, w_key, w_value, d_attended):
    zs, ys, _, xs = GRID
    _, slots, block_rows, width_in = tile_embed.shape
    rows = slots * block_rows
    latents, width = queries.shape
    core = lax.axis_index("c")
    first = core == 0
    both_rows = 2 * rows
    big_flops = 2 * both_rows * width_in * width
    core_arg = core.astype(jnp.int32)[None]
    rep_arg = lax.axis_index("x").astype(jnp.int32)[None]
    anywhere = pl.BlockSpec(memory_space=pl.ANY)
    in_vmem = pl.BlockSpec(memory_space=pltpu.VMEM)
    in_hbm = pl.BlockSpec(memory_space=pltpu.HBM)

    def partner(value):
        return lax.ppermute(value, "c", [(0, 1), (1, 0)])

    def shifted(value, by):
        return lax.ppermute(value, "x", [(x, (x + by) % xs) for x in range(xs)])

    key_half = jnp.where(first, w_key[:, :HALF], w_key[:, HALF:])
    value_half = jnp.where(first, w_value[:, :HALF], w_value[:, HALF:])
    w_own = jnp.concatenate([key_half, value_half[:, 256:], value_half[:, :256]], axis=1)
    w_parts = [w_own, shifted(w_own, -1)]
    q_scaled = (queries.astype(jnp.float32) * SCORE_SCALE).astype(jnp.bfloat16)

    x_own = tile_embed.reshape(rows, width_in)
    x_part = partner(x_own)
    limits = jnp.where(block_slide[0] >= 0, tile_count[0, 0] - block_rank[0] * block_rows, 0)
    limits2 = partner(limits)

    def turned(tiles, after, name):
        return call(
            lambda *refs: turn_kernel(*refs, zs=zs, ys=ys), name, 1, (5,), [in_vmem, anywhere],
            (row_block(width_in // 5, rows), whole((8, LANES))), (pltpu.HBM((width_in, rows), jnp.bfloat16), shaped((8, LANES), jnp.float32)),
            2 * rows * width_in * width_in, 5 << 20, (), FORWARD_LIMIT,
        )(core_arg, tiles, after)

    turned_own, own_done = turned(x_own, q_scaled, "turn_own")
    if xs == 4:
        passed, own_done = lax.optimization_barrier((w_parts[1], own_done))
        w_parts = [w_own, passed, shifted(passed, -1), shifted(w_own, 1)]
    turned_part, part_done = turned(x_part, own_done, "turn_partner")

    stat_shape = (latents, 1, 3 * LANES)
    kv, stats = call(
        lambda *refs: forward_kernel(*refs, block_rows=block_rows, reps=xs), "forward_pass", 4, (1,),
        [in_vmem, in_hbm, *[in_vmem] * xs, in_vmem, in_vmem], (in_vmem, in_vmem),
        (shaped((both_rows, width)), shaped(stat_shape, jnp.float32)), big_flops, 10 << 20,
        [
            pltpu.VMEM((width_in, width), jnp.bfloat16), pltpu.VMEM((rows, width_in), jnp.bfloat16),
            pltpu.SemaphoreType.DMA((1,)),
        ],
        FORWARD_LIMIT,
    )(core_arg, rep_arg, limits, limits2, x_own, x_part, *w_parts, q_scaled, part_done)

    chips = ("z", "y")
    stats = lax.all_to_all(stats, chips, 0, 0, tiled=True)
    merged = call(
        lambda *refs: combine_kernel(*refs, sources=zs * ys), "combine", 0, (1,),
        [in_vmem], in_vmem, shaped(stat_shape, jnp.float32), stats.size * 4, stats.size * 4, (), FORWARD_LIMIT,
    )(stats)
    merged = lax.all_to_all(merged, chips, 0, 0, tiled=True)

    d_out = d_attended.reshape(latents, width)
    turned_own, turned_part = (pltpu.with_memory_space_constraint(part, pltpu.HBM) for part in (turned_own, turned_part))
    attended, grads = call(
        lambda *refs: backward_kernel(*refs, block_rows=block_rows), "backward_pass", 3, (2,),
        [in_hbm, in_hbm, in_vmem, in_vmem, whole(d_out.shape), in_vmem],
        (whole((latents, 3 * LANES)), row_block(width_in // 2, width)),
        (shaped((latents, 3 * LANES)), shaped((width_in, width))),
        big_flops, 10 << 20,
        [
            pltpu.VMEM((both_rows, width), jnp.bfloat16), pltpu.VMEM((2, width_in, rows), jnp.bfloat16),
            pltpu.SemaphoreType.DMA((2,)),
        ],
        BACKWARD_LIMIT,
    )(core_arg, limits, limits2, turned_own, turned_part, kv, q_scaled, d_out, merged)
    mine = attended[:, :HALF]
    theirs = partner(mine)
    attended = jnp.where(first, jnp.concatenate([mine, theirs], axis=1), jnp.concatenate([theirs, mine], axis=1))

    received = lax.all_to_all(grads, AXES, 0, 0, axis_index_groups=first_groups(), tiled=True)
    received = received.reshape(zs, width_in // zs, width)
    length = width_in // (2 * zs * ys)
    share = width // xs
    chunk = (ys * xs, padded_to(length, 16), padded_to(2 * share, LANES))
    pieces = call(
        lambda *refs: fold_kernel(*refs, length=length, reps=xs), "fold", 0, (1,), [whole(received.shape)],
        whole(chunk), shaped(chunk), received.size, received.size * 2, (), FORWARD_LIMIT,
    )(received)
    received = lax.all_to_all(pieces, AXES, 0, 0, axis_index_groups=second_groups(), tiled=True)
    total = jnp.sum(received.astype(jnp.float32), axis=0)[:length, : 2 * share]
    half = xs // 2
    home = [(c * xs + x, (x // half) * xs + c * half + x % half) for c in range(2) for x in range(xs)]
    total = lax.ppermute(total, ("c", "x"), home)
    return (attended.reshape(1, 1, latents, width), total[:, :share], total[:, share:])


def solution(mesh):
    grid = Mesh(mesh.devices.reshape(GRID), AXES)
    placed = (
        P("x", TILES, None, None),
        P("x", TILES),
        P("x", TILES),
        P("x", None),
        P(),
        P("x", None),
        P("x", None),
        P("x", None, None, None),
    )
    return jax.shard_map(
        body,
        mesh=grid,
        in_specs=placed,
        out_specs=(P("x", None, None, None), P(TILES, "x"), P(TILES, "x")),
        check_vma=False,
    )
```
